32 devices in a mesh: groups: 2 (over x), ctx: 16 (over z, y, core).
Axes of the slice: x: 2, y: 2, z: 4, core: 2. Of those that a mesh axis runs over, the one named last changes fastest.
Arguments:
- query_latent: bfloat16 [96, 8192], P(('groups', 'ctx')), parts along dimension 0, may hold values from -512 to 512
- query_rope: bfloat16 [96, 1024], P(('groups', 'ctx')), parts along dimension 0, may hold values from -18 to 18
- cache_latent: bfloat16 [16384, 512], P(('groups', 'ctx')), parts along dimension 0, may hold values from -4 to 4
- cache_rope: bfloat16 [128, 8192], P('groups', 'ctx'), parts along dimension 0, may hold values from -4 to 4
- valid_len: int32 [96], P('groups'), parts along dimension 0, may hold values from 2048 to 8192
- w_vo: bfloat16 [8192, 2560], P('ctx'), may hold values from -0.29882812 to 0.29882812
- residual: bfloat16 [96, 2560], P(('groups', 'ctx')), parts along dimension 0, may hold values from -6 to 6
- norm_gain: float32 [2560], replicated, may hold values from 0.25 to 1.75
- expert_ids: int32 [96, 6], P('groups'), parts along dimension 0, may hold values from 0 to 15, all different within a row; in each aligned block of 48 rows (0 to 47, 48 to 95, ...) at most 36 rows name the same one
- route_weight: float32 [96, 6], P('groups'), parts along dimension 0, may hold values from 0.1 to 0.4
- w_gate: bfloat16 [16, 2560, 768], P('ctx'), may hold values from -0.125 to 0.125
- w_up: bfloat16 [16, 2560, 768], P('ctx'), may hold values from -0.125 to 0.125
- w_down: bfloat16 [16, 768, 2560], P('ctx'), may hold values from -0.21875 to 0.21875
Outputs:
- attn_out: bfloat16 [96, 2560], P(('groups', 'ctx')), parts along dimension 0
- layer_out: bfloat16 [96, 2560], P(('groups', 'ctx')), parts along dimension 0
The draws below stay inside these ranges and needn't reach their ends.
There are 2 independent parts, one for each index of `groups`. The reference program is written for one: setup_inputs(seed, part) draws one part's arguments, and reference() takes and returns one part's arrays. A program takes and returns all parts, laid end to end along the dimension named above; an argument that names none is the same for every part. Nothing has to cross between parts.
Inputs may be any that keep to these rules, and one draw needn't show every extreme that they name: `expert_ids`: each row names 6 different experts; no expert is named by more than 36 rows, a bound that some block reaches.
All inputs are finite; a program needn't handle non-finite values.
Results may differ from the reference program's by a relative error of at most 0.006.
Values may be sent and summed in bfloat16 or wider, within the bound.
No kernel may reach another device: no remote copies, remote signals or barrier semaphores. Data moves between devices by JAX's collectives and lax.ppermute only.
A program may use at most 128 MiB of HBM per device.

```python
import math
import jax
import jax.numpy as jnp
import numpy as np
from jax import lax

D = 2560
H = 16
LAT = 512
ROPE = 64
FFE = 768
TOP = 6
CTX_DEV = 512
ROWS = 48
CTX = 8192
EXPERTS = 16
CAP = 36
N_CTX = 16


softmax_scale = 192.0 ** (-0.5)


aligned_pairs = 8


gap_target = 2.0


lowest_target = 120.0


highest_target = 360.0


def cache_parts(key):
    base_key = jax.random.fold_in(key, 11)
    latent = jnp.clip(jax.random.normal(jax.random.fold_in(base_key, 1), (CTX, LAT), jnp.float32), -4.0, 4.0)
    rope_keys = jnp.clip(jax.random.normal(jax.random.fold_in(base_key, 2), (ROPE, CTX), jnp.float32), -4.0, 4.0)
    return (latent, rope_keys)


def draw_cache_latent(key, part):
    return cache_parts(key)[0].astype(jnp.bfloat16)


def draw_cache_rope(key, part):
    return cache_parts(key)[1].astype(jnp.bfloat16)


def query_parts(key):
    latent, rope_keys = cache_parts(key)
    latent = latent.astype(jnp.bfloat16).astype(jnp.float32)
    rope_keys = rope_keys.astype(jnp.bfloat16).astype(jnp.float32)
    base_key = jax.random.fold_in(key, 23)
    query_lat = 1.5 * jnp.clip(jax.random.normal(jax.random.fold_in(base_key, 1), (ROWS, H, LAT), jnp.float32), -6.0, 6.0)
    query_rot = 1.5 * jnp.clip(jax.random.normal(jax.random.fold_in(base_key, 2), (ROWS, H, ROPE), jnp.float32), -6.0, 6.0)
    query_rot = query_rot.astype(jnp.bfloat16).astype(jnp.float32)
    window = CTX // 4
    first_index = jax.random.randint(jax.random.fold_in(base_key, 4), (aligned_pairs,), 0, window)
    second_index = (first_index + jax.random.randint(jax.random.fold_in(base_key, 5), (aligned_pairs,), 1, window)) % window
    pair_rows = jnp.arange(aligned_pairs) * (ROWS // aligned_pairs)
    pair_heads = jnp.arange(aligned_pairs) % H
    strength = jnp.linspace(lowest_target, highest_target, aligned_pairs) / (softmax_scale * LAT)
    first_key = latent[first_index]
    second_key = latent[second_index]
    first_rope = jnp.transpose(rope_keys[:, first_index])
    second_rope = jnp.transpose(rope_keys[:, second_index])
    pair_rope = query_rot[pair_rows, pair_heads]
    stretch = strength * jnp.sum(first_key * (first_key - second_key), axis=1) + jnp.sum(pair_rope * (first_rope - second_rope), axis=1) - gap_target / softmax_scale
    direction = second_key / jnp.sum(second_key * (second_key - first_key), axis=1, keepdims=True)
    aligned = strength[:, None] * first_key + stretch[:, None] * direction
    query_lat = query_lat.at[pair_rows, pair_heads].set(aligned)
    return (query_lat.reshape(ROWS, H * LAT), query_rot.reshape(ROWS, H * ROPE))


def draw_query_latent(key, part):
    return query_parts(key)[0].astype(jnp.bfloat16)


def draw_query_rope(key, part):
    return query_parts(key)[1].astype(jnp.bfloat16)


def set_ends(entries, own_key, low, largest):
    shape = entries.shape
    spot = [jax.random.randint(jax.random.fold_in(own_key, axis), (), 0, shape[axis]) for axis in range(len(shape))]
    entries = entries.at[tuple(spot)].set(low)
    longest = shape.index(max(shape))
    spot[longest] = (spot[longest] + 1) % shape[longest]
    return entries.at[tuple(spot)].set(largest)


def levels(own_key, shape, split, low, top_value):
    def one(dim, parts):
        draws = jax.random.uniform(jax.random.fold_in(jax.random.fold_in(own_key, 6), dim), (parts,), jnp.float32, low / len(split), top_value / len(split))
        return jnp.repeat(jnp.exp(draws), shape[dim] // parts).reshape((-1,) + (1,) * (len(shape) - dim - 1))

    level = one(*split[0])
    for cut in split[1:]:
        level = level * one(*cut)
    return level


def routed_block(own_key, own, number, rows, count, top, most, skew):
    sequence = jax.random.permutation(own_key, count)
    packed, usual = portions_of(count, rows * top, most, skew, True), portions_of(count, rows * top, most, skew, False)
    places = jnp.arange(count)

    def named(lengths, offset_by):
        used = int((lengths > 0).sum())
        fixed = max(1, used // 4)
        moved = fixed + (places - fixed + offset_by * (used - fixed)) % max(1, count - fixed)
        return jnp.zeros((count,), jnp.int32).at[sequence[jnp.where(places < fixed, places, moved)]].set(jnp.asarray(lengths, jnp.int32))

    lengths = jnp.where(number % 4 == 0, named(packed, number // 4), named(usual, number - number // 4 - 1))
    mixed = jax.random.permutation(jax.random.fold_in(own, 3), count)
    donor, receiver = mixed[0:count // 2 * 2:2], mixed[1:count // 2 * 2:2]
    margin = jnp.minimum(lengths[donor] - 1, most - lengths[receiver]) // 2
    margin = jnp.where((donor == sequence[0]) | (receiver == sequence[0]) | (lengths[receiver] == 0), 0, jnp.maximum(margin, 0))
    moved = jax.random.randint(jax.random.fold_in(own, 4), (count // 2,), 0, 1 << 20) % (margin + 1)
    lengths = lengths.at[donor].add(-moved).at[receiver].add(moved)
    items = jnp.searchsorted(jnp.cumsum(lengths), jnp.arange(rows * top), side="right").astype(jnp.int32)
    grid = items.reshape(top, rows).T
    grid = grid[jax.random.permutation(jax.random.fold_in(own, 1), rows)]
    offset_by = jax.random.randint(jax.random.fold_in(own, 2), (rows, 1), 0, top)
    return jnp.take_along_axis(grid, (jnp.arange(top)[None, :] + offset_by) % top, axis=1)


def portions_of(count, total, most, skew, full):
    portions = [(1 << 20) // math.isqrt(rank ** skew) + 1 for rank in range(1, count + 1)]
    largest = most if full else min(most, max(-(-total // count), total * portions[0] // sum(portions)))
    least = 1 if total - largest >= count - 1 else 0
    counts, spare = [largest] + [least] * (count - 1), total - largest - least * (count - 1)
    while spare > 0:
        candidates = [i for i in range(1, count) if counts[i] < largest] or [i for i in range(1, count) if counts[i] < most]
        whole, left = sum([portions[i] for i in candidates]), spare
        for i in candidates:
            extra = min(most - counts[i], max(1, left * portions[i] // whole), spare)
            counts[i] = counts[i] + extra
            spare = spare - extra
    return np.array(counts)


def normal_values(key, extent, deviation, bound, cuts=(), kind=jnp.bfloat16):
    loudness = levels(key, extent, cuts, -0.22, 0.18) if cuts else 1.0
    drawn = jax.random.normal(key, extent, jnp.float32) * deviation * loudness
    return jnp.minimum(jnp.maximum(drawn, -bound), bound).astype(kind)


def setup_inputs(seed: int = 0, part: int = 0) -> dict:
    arg_keys = jax.random.split(jax.random.key(seed), 14)
    part_splits = jax.random.split(jax.random.fold_in(arg_keys[13], part), 14)
    query_latent = draw_query_latent(jax.random.fold_in(jax.random.fold_in(arg_keys[13], part), 71), part)
    query_rope = draw_query_rope(jax.random.fold_in(jax.random.fold_in(arg_keys[13], part), 71), part)
    cache_latent = draw_cache_latent(jax.random.fold_in(jax.random.fold_in(arg_keys[13], part), 71), part)
    cache_rope = draw_cache_rope(jax.random.fold_in(jax.random.fold_in(arg_keys[13], part), 71), part)
    valid_len = set_ends(jax.random.randint(part_splits[4], (ROWS,), CTX // 4, CTX + 1), jax.random.fold_in(part_splits[4], 1), CTX // 4, CTX).astype(jnp.int32)
    w_vo = normal_values(arg_keys[5], (H * LAT, D), 0.05, 0.29882812, ((0, 16),))
    residual = normal_values(part_splits[6], (ROWS, D), 1.0, 6.0, ((0, 16),))
    norm_gain = jnp.clip(1.0 + 0.15 * jax.random.normal(arg_keys[7], (D,), jnp.float32), 0.25, 1.75)
    expert_ids_keys = jax.random.split(jax.random.fold_in(part_splits[8], 1), ROWS // ROWS)
    expert_ids_turns = jax.random.permutation(jax.random.fold_in(part_splits[8], 3), ROWS // ROWS)
    expert_ids = jax.vmap(lambda own, number: routed_block(jax.random.fold_in(part_splits[8], 2), own, number, ROWS, EXPERTS, TOP, CAP, 2))(expert_ids_keys, expert_ids_turns).reshape((ROWS, TOP))
    route_weight = jnp.clip(jax.random.uniform(part_splits[9], (ROWS, TOP), jnp.float32, 0.1, 0.4), 0.1, 0.4)
    w_gate = normal_values(arg_keys[10], (EXPERTS, D, FFE), D ** -0.5, 0.125, ((0, 16),))
    w_up = normal_values(arg_keys[11], (EXPERTS, D, FFE), D ** -0.5, 0.125, ((0, 16),))
    w_down = normal_values(arg_keys[12], (EXPERTS, FFE, D), FFE ** -0.5, 0.21875, ((0, 16),))
    return {"query_latent": query_latent, "query_rope": query_rope, "cache_latent": cache_latent, "cache_rope": cache_rope, "valid_len": valid_len, "w_vo": w_vo, "residual": residual, "norm_gain": norm_gain, "expert_ids": expert_ids, "route_weight": route_weight, "w_gate": w_gate, "w_up": w_up, "w_down": w_down}


softmax_scale = 192.0 ** (-0.5)
negative_fill = -1e+30
norm_eps = 1e-06

def expert_apply(inputs, gate_weight, up_weight, down_weight):
    gate_out = jnp.dot(inputs, gate_weight, preferred_element_type=jnp.float32)
    up_out = jnp.dot(inputs, up_weight, preferred_element_type=jnp.float32)
    hidden = (jax.nn.silu(gate_out) * up_out).astype(jnp.bfloat16)
    return jnp.dot(hidden, down_weight, preferred_element_type=jnp.float32).astype(jnp.bfloat16)

def reference(query_latent, query_rope, cache_latent, cache_rope, valid_len, w_vo, residual, norm_gain, expert_ids, route_weight, w_gate, w_up, w_down):
    flat_query = query_latent.reshape(ROWS * H, LAT)
    flat_rope = query_rope.reshape(ROWS * H, ROPE)
    limit = jnp.repeat(valid_len, H)[:, None]
    latent_blocks = cache_latent.reshape(N_CTX, CTX_DEV, LAT)
    rope_blocks = jnp.transpose(cache_rope.reshape(ROPE, N_CTX, CTX_DEV), (1, 0, 2))

    def attend(carry, block):
        accumulated, summed, highest = carry
        latent_block, rope_block, block_index = block
        scores = lax.dot_general(flat_query, latent_block, (((1,), (1,)), ((), ())), preferred_element_type=jnp.float32)
        scores = (scores + jnp.dot(flat_rope, rope_block, preferred_element_type=jnp.float32)) * softmax_scale
        position = block_index * CTX_DEV + lax.broadcasted_iota(jnp.int32, (1, CTX_DEV), 1)
        usable = position < limit
        block_max = lax.optimization_barrier(jnp.max(jnp.where(usable, scores, negative_fill), axis=1))
        weights = jnp.where(usable, jnp.exp(scores - block_max[:, None]), 0.0).astype(jnp.bfloat16)
        block_sum = lax.optimization_barrier(jnp.sum(weights.astype(jnp.float32), axis=1))
        block_out = jnp.dot(weights, latent_block, preferred_element_type=jnp.float32)
        running_max = jnp.maximum(highest, block_max)
        retain = jnp.exp(highest - running_max)
        renewed = jnp.exp(block_max - running_max)
        accumulated = accumulated * retain[:, None] + block_out * renewed[:, None]
        summed = summed * retain + block_sum * renewed
        return ((accumulated, summed, running_max), None)
    initial = (jnp.zeros((ROWS * H, LAT), jnp.float32), jnp.zeros((ROWS * H,), jnp.float32), jnp.full((ROWS * H,), negative_fill, jnp.float32))
    (accumulated, summed, highest), unused = lax.scan(attend, initial, (latent_blocks, rope_blocks, jnp.arange(N_CTX, dtype=jnp.int32)))
    attention = (accumulated / summed[:, None]).astype(jnp.bfloat16).reshape(ROWS, H * LAT)
    projected = jnp.dot(attention, w_vo, preferred_element_type=jnp.float32)
    hidden_state = residual.astype(jnp.float32) + projected
    normed = (hidden_state * lax.rsqrt(lax.optimization_barrier(jnp.mean(hidden_state * hidden_state, axis=1, keepdims=True)) + norm_eps) * norm_gain).astype(jnp.bfloat16)
    expert_iota = lax.broadcasted_iota(jnp.int32, (1, 1, EXPERTS), 2)
    route_table = lax.optimization_barrier(jnp.sum(jnp.where(expert_ids[:, :, None] == expert_iota, route_weight[:, :, None], 0.0), axis=1))
    slot_iota = lax.broadcasted_iota(jnp.int32, (CAP, 1), 0)

    def visit(mixture, block):
        gate_weight, up_weight, down_weight, expert = block
        weight_col = lax.dynamic_slice_in_dim(route_table, expert, 1, 1)
        chosen = weight_col[:, 0] > 0.0
        slot_index = jnp.where(chosen, jnp.cumsum(chosen.astype(jnp.int32)) - 1, -1).astype(jnp.int32)
        picker = (slot_index[None, :] == slot_iota).astype(jnp.bfloat16)
        picked = jnp.dot(picker, normed, preferred_element_type=jnp.float32).astype(jnp.bfloat16)
        result = expert_apply(picked, gate_weight, up_weight, down_weight)
        placed = lax.dot_general(picker, result, (((0,), (0,)), ((), ())), preferred_element_type=jnp.float32)
        return (mixture + weight_col * placed, None)
    mixture, unused = lax.scan(visit, jnp.zeros((ROWS, D), jnp.float32), (w_gate, w_up, w_down, jnp.arange(EXPERTS, dtype=jnp.int32)))
    layer_out = (hidden_state + mixture).astype(jnp.bfloat16)
    return (projected.astype(jnp.bfloat16), layer_out)
```

```python
import functools

import jax
import jax.numpy as jnp
import numpy as np
from jax import lax
from jax.experimental import pallas as pl
from jax.experimental.pallas import tpu as pltpu
from jax.sharding import PartitionSpec as P


softmax_scale = 192.0 ** (-0.5)
negative_fill = -1e30
norm_eps = 1e-06
share = 4
strip = 512

VMEM = pltpu.VMEM
SMEM = pltpu.SMEM
f32 = jnp.float32
bf16 = jnp.bfloat16


def expert_apply(inputs, gate_weight, up_weight, down_weight):
    gate_out = jnp.dot(inputs, gate_weight, preferred_element_type=jnp.float32)
    up_out = jnp.dot(inputs, up_weight, preferred_element_type=jnp.float32)
    hidden = (jax.nn.silu(gate_out) * up_out).astype(jnp.bfloat16)
    return jnp.dot(hidden, down_weight, preferred_element_type=jnp.float32).astype(jnp.bfloat16)


def plain_layer(
    query_latent,
    query_rope,
    cache_latent,
    cache_rope,
    valid_len,
    w_vo,
    residual,
    norm_gain,
    expert_ids,
    route_weight,
    w_gate,
    w_up,
    w_down,
):
    query_all, rope_all = (
        lax.all_gather(query_latent, "ctx", axis=0, tiled=True),
        lax.all_gather(query_rope, "ctx", axis=0, tiled=True),
    )
    total_rows = query_all.shape[0]
    own_rows = residual.shape[0]
    latent = cache_latent.shape[1]
    rope_dim = cache_rope.shape[0]
    head_count = rope_all.shape[1] // rope_dim
    block_len = cache_latent.shape[0]
    devices = lax.axis_size("ctx")
    self_index = lax.axis_index("ctx")
    col_count = head_count * latent // devices
    flat_query = query_all.reshape(total_rows * head_count, latent)
    flat_rope = rope_all.reshape(total_rows * head_count, rope_dim)
    scores = lax.dot_general(
        flat_query, cache_latent, (((1,), (1,)), ((), ())), preferred_element_type=jnp.float32
    )
    scores = (
        scores + jnp.dot(flat_rope, cache_rope, preferred_element_type=jnp.float32)
    ) * softmax_scale
    position = self_index * block_len + lax.broadcasted_iota(jnp.int32, (1, block_len), 1)
    usable = position < jnp.repeat(valid_len, head_count)[:, None]
    block_max = jnp.max(jnp.where(usable, scores, negative_fill), axis=1)
    weights = jnp.where(usable, jnp.exp(scores - block_max[:, None]), 0.0).astype(jnp.bfloat16)
    block_sum = jnp.sum(weights.astype(jnp.float32), axis=1)
    block_out = jnp.dot(weights, cache_latent, preferred_element_type=jnp.float32)
    row_max = block_max.reshape(total_rows, head_count)
    row_sum = block_sum.reshape(total_rows, head_count)
    global_max = lax.pmax(row_max, "ctx")
    factor = jnp.exp(row_max - global_max)
    scaled = (block_out.reshape(total_rows, head_count, latent) * factor[:, :, None]).reshape(
        total_rows, head_count * latent
    )
    merged = lax.psum_scatter(scaled, "ctx", scatter_dimension=1, tiled=True)
    totals = lax.psum(row_sum * factor, "ctx")
    divisor = lax.dynamic_slice_in_dim(totals, self_index * col_count // latent, 1, 1)
    attention = (merged / divisor).astype(jnp.bfloat16)
    projected = lax.psum_scatter(
        jnp.dot(attention, w_vo, preferred_element_type=jnp.float32),
        "ctx",
        scatter_dimension=0,
        tiled=True,
    )
    hidden_state = residual.astype(jnp.float32) + projected
    normed = (
        hidden_state
        * lax.rsqrt(jnp.mean(hidden_state * hidden_state, axis=1, keepdims=True) + norm_eps)
        * norm_gain
    ).astype(jnp.bfloat16)
    expert_iota = lax.broadcasted_iota(jnp.int32, (1, 1, devices), 2)
    route_table = jnp.sum(
        jnp.where(expert_ids[:, :, None] == expert_iota, route_weight[:, :, None], 0.0), axis=1
    )
    gate_own = w_gate[0]
    up_own = w_up[0]
    down_own = w_down[0]
    own_table = jnp.transpose(
        lax.dynamic_slice_in_dim(route_table, self_index * own_rows, own_rows, 0)
    )
    outgoing = jnp.where(
        own_table[:, :, None] > 0.0, normed[None, :, :], jnp.zeros((), jnp.bfloat16)
    )
    arrived = lax.all_to_all(outgoing, "ctx", split_axis=0, concat_axis=0, tiled=True)
    item_count = arrived.shape[1]
    stacked = arrived.reshape(devices * item_count, arrived.shape[2])
    result = expert_apply(stacked, gate_own, up_own, down_own).reshape(
        devices, item_count, arrived.shape[2]
    )
    returned = lax.all_to_all(result, "ctx", split_axis=0, concat_axis=0, tiled=True)
    mixture = jnp.sum(own_table[:, :, None] * returned.astype(jnp.float32), axis=0)
    layer_out = (hidden_state + mixture).astype(jnp.bfloat16)
    return (projected.astype(jnp.bfloat16), layer_out)


def call(kernel, out_shape, *operands, spaces=None, scratch=(), limit=24, cost=None):
    spaces = spaces or {}
    in_specs = [pl.BlockSpec(memory_space=spaces.get(i, VMEM)) for i in range(len(operands))]
    many = isinstance(out_shape, (tuple, list))
    out_specs = [pl.BlockSpec(memory_space=VMEM) for _ in out_shape] if many else pl.BlockSpec(memory_space=VMEM)
    return pl.pallas_call(
        kernel,
        out_shape=out_shape,
        in_specs=in_specs,
        out_specs=out_specs,
        scratch_shapes=list(scratch),
        compiler_params=pltpu.CompilerParams(vmem_limit_bytes=limit << 20),
        cost_estimate=cost,
    )(*operands)


def query_order(rows, devices, heads_each, total_rows):
    per = rows * heads_each
    target = np.zeros((2, heads_each * total_rows, 3 * devices * 8), np.float32)
    rope = np.zeros((2, heads_each * total_rows, devices * 8), np.float32)
    for source in range(devices):
        for unit in range(2 * per):
            half, item = divmod(unit, per)
            row, head = divmod(item, heads_each)
            column = (unit // 8) * devices * 8 + source * 8 + unit % 8
            target[half, head * total_rows + source * rows + row, column] = 1.0
        for item in range(per):
            row, head = divmod(item, heads_each)
            rope[item // 8, head * total_rows + source * rows + row, source * 8 + item % 8] = 1.0
    flat = 2 * heads_each * total_rows
    return (
        jnp.asarray(target.reshape(flat, -1), bf16),
        jnp.asarray(rope.reshape(flat, -1), bf16),
    )


def strip_order(rows, devices, strips, height):
    order = np.zeros((devices * height, strips * rows * devices), np.float32)
    for device in range(devices):
        for row in range(rows):
            for part in range(strips):
                order[device * height + row * strips + part, part * rows * devices + device * rows + row] = 1.0
    return order


def pack_queries(rows, heads_each, latent, rope_dim, query_ref, rope_ref, out_ref, piece, rope_piece):
    per = rows * heads_each
    half_width = latent // 2
    groups = out_ref.shape[0] // share
    query = query_ref[...].astype(f32)
    rope = rope_ref[...].astype(f32)
    lane = lax.broadcasted_iota(jnp.int32, (8, 128), 1)
    rope_piece[...] = jnp.zeros_like(rope_piece)
    for place in range(share):
        for item in range(per):
            row, index = divmod(item, heads_each)
            head = share * index + place
            for half in range(2):
                begin = head * latent + half * half_width
                piece[place, half * per + item : half * per + item + 1, :] = query[row : row + 1, begin : begin + half_width]
            block = head * rope_dim // 128
            rope_piece[place, item : item + 1, :] = rope[row : row + 1, block * 128 : (block + 1) * 128]
    for place in range(share):
        first = rope_piece[place, 0:8, :]
        second = rope_piece[place, 8:16, :]
        if place % 2 == 1:
            first = pltpu.roll(first, 64, 1)
        else:
            second = pltpu.roll(second, 64, 1)
        tail = jnp.where(lane < 64, first, second).astype(bf16)
        tiles = []
        for rt in range(2 * per // 8):
            for lt in range(half_width // 128):
                tiles.append(piece[place, rt * 8 : (rt + 1) * 8, lt * 128 : (lt + 1) * 128].astype(bf16))
        tiles.append(tail)
        for group in range(groups):
            for index, tile in enumerate(tiles):
                out_ref[group * share + place, index] = tile


def attend(rows, heads_each, block_len, latent, arrived_ref, order_ref, rope_order_ref, length_ref, own_ref, core_ref, near_ref, far_ref, out_ref, limit_ref, scores_ref):
    devices = arrived_ref.shape[0]
    total_rows = rows * devices
    flat = heads_each * total_rows
    me = lax.axis_index("ctx")
    row_tiles = 2 * rows * heads_each // 8
    for row in range(total_rows):
        limit_ref[row : row + 1, :] = jnp.full((1, 128), length_ref[row], jnp.int32)
    gathered = jnp.concatenate(
        [
            jnp.concatenate(
                [arrived_ref[:, 2 * rt + lt].reshape(devices * 8, 128) for lt in range(2)], axis=1
            )
            for rt in range(row_tiles)
        ],
        axis=0,
    )
    ordered = jnp.dot(order_ref[...], gathered, preferred_element_type=f32).astype(bf16)
    query = jnp.concatenate([ordered[:flat], ordered[flat:]], axis=1)
    rope_rows = arrived_ref[:, 2 * row_tiles].reshape(devices * 8, 128)
    rope_ordered = jnp.dot(rope_order_ref[...], rope_rows, preferred_element_type=f32).astype(bf16)
    rope_query = jnp.concatenate([rope_ordered[:flat], rope_ordered[flat:]], axis=1)
    blocks = (own_ref, core_ref, near_ref, far_ref)
    limits = limit_ref[...][:, 0:1]
    column = lax.broadcasted_iota(jnp.int32, (total_rows, block_len), 1)
    highest = None
    usable = []
    for index, block in enumerate(blocks):
        begin = lax.bitwise_xor(me, index) * block_len
        valid = column + begin < limits
        keys = block[0:latent, :]
        rope_keys = block[latent:, :]
        empty = jnp.zeros_like(rope_keys)
        rope_keys = jnp.concatenate([rope_keys, empty, empty, rope_keys], axis=0)
        scores = lax.dot_general(query, keys, (((1,), (1,)), ((), ())), preferred_element_type=f32)
        scores = (scores + jnp.dot(rope_query, rope_keys, preferred_element_type=f32)) * softmax_scale
        scores = jnp.where(valid[None], scores.reshape(heads_each, total_rows, block_len), negative_fill).reshape(flat, block_len)
        scores_ref[index] = scores
        top = jnp.max(scores, axis=1, keepdims=True)
        highest = top if highest is None else jnp.maximum(highest, top)
        usable.append(valid)
    total = None
    summed = None
    for index, block in enumerate(blocks):
        weights = jnp.exp(scores_ref[index] - highest)
        weights = jnp.where(usable[index][None], weights.reshape(heads_each, total_rows, block_len), 0.0).reshape(flat, block_len)
        weights = weights.astype(bf16)
        part = jnp.sum(weights.astype(f32), axis=1, keepdims=True)
        summed = part if summed is None else summed + part
        part = jnp.dot(weights, block[0:latent, :], preferred_element_type=f32)
        total = part if total is None else total + part
    lane = lax.broadcasted_iota(jnp.int32, (8, 128), 1)
    for head in range(heads_each):
        base = head * total_rows
        out_ref[head, 0:total_rows, :] = total[base : base + total_rows].astype(bf16)
        note = jnp.zeros((8, 128), f32)
        for tile in range(total_rows // 8):
            for offset, value in ((0, highest), (3, summed)):
                value = jnp.broadcast_to(value[base + tile * 8 : base + tile * 8 + 8], (8, 128))
                for piece in range(3):
                    rounded = value.astype(bf16).astype(f32)
                    note = jnp.where(lane == 8 * tile + offset + piece, rounded, note)
                    value = value - rounded
        wide = jnp.concatenate([note, jnp.zeros((8, out_ref.shape[2] - 128), f32)], axis=1)
        out_ref[head, total_rows:, :] = wide.astype(bf16)


def merge_project(arrived_ref, weight_ref, order_ref, out_ref, attention_ref):
    sources, height, latent = arrived_ref.shape
    total_rows = height - 8
    peaks = []
    sums = []
    for source in range(sources):
        note = arrived_ref[source, total_rows:, 0:128].astype(f32)
        shifted = [note] + [pltpu.roll(note, 128 - step, 1) for step in range(1, 6)]
        peaks.append(shifted[0] + shifted[1] + shifted[2])
        sums.append(shifted[3] + shifted[4] + shifted[5])
    highest = functools.reduce(jnp.maximum, peaks)
    factors = [jnp.exp(peak - highest) for peak in peaks]
    divisor = sum(factor * part for factor, part in zip(factors, sums))
    factors = [factor / divisor for factor in factors]
    for tile in range(total_rows // 8):
        span = slice(tile * 8, tile * 8 + 8)
        attention_ref[span, :] = sum(
            factor[:, 8 * tile : 8 * tile + 1] * arrived_ref[source, span, :].astype(f32)
            for source, factor in enumerate(factors)
        )
    attention = attention_ref[...].astype(bf16)
    send_rows(attention, weight_ref, order_ref, out_ref)


def send_rows(left, weight_ref, order_ref, out_ref):
    strips = weight_ref.shape[1] // strip
    parts = [
        jnp.dot(left, weight_ref[:, part * strip : (part + 1) * strip], preferred_element_type=f32).astype(bf16)
        for part in range(strips)
    ]
    stacked = jnp.concatenate(parts, axis=0)
    ordered = jnp.dot(order_ref[...], stacked, preferred_element_type=f32).astype(bf16)
    out_ref[...] = ordered.reshape(out_ref.shape)


def norm_rows(arrived_ref, residual_ref, gain_ref, attn_ref, hidden_ref, out_ref, natural, stripped):
    rows, width = residual_ref.shape
    strips = width // strip
    summed = jnp.sum(arrived_ref[...].astype(f32), axis=0)
    for row in range(rows):
        for part in range(strips):
            at = row * strips + part
            natural[row : row + 1, part * strip : (part + 1) * strip] = summed[at : at + 1]
    projected = natural[0:rows, :]
    attn_ref[...] = projected.astype(bf16)
    hidden = residual_ref[...].astype(f32) + projected
    hidden_ref[...] = hidden
    normed = hidden * lax.rsqrt(jnp.mean(hidden * hidden, axis=1, keepdims=True) + norm_eps) * gain_ref[...]
    stripped[...] = jnp.zeros_like(stripped)
    for row in range(rows):
        for part in range(strips):
            at = row * strips + part
            stripped[at : at + 1, :] = normed[row : row + 1, part * strip : (part + 1) * strip]
    tile = stripped[...].astype(bf16)
    for device in range(out_ref.shape[0]):
        out_ref[device] = tile


def run_expert(arrived_ref, back_ref, order_ref, gate_ref, up_ref, down_ref, out_ref):
    devices, height, _ = arrived_ref.shape
    strips = gate_ref.shape[0] // strip
    pieces = arrived_ref[...].reshape(devices * height, strip)
    ordered = jnp.dot(back_ref[...], pieces, preferred_element_type=f32).astype(bf16)
    total_rows = ordered.shape[0] // strips
    inputs = jnp.concatenate([ordered[part * total_rows : (part + 1) * total_rows] for part in range(strips)], axis=1)
    gate = jnp.dot(inputs, gate_ref[...], preferred_element_type=f32)
    up = jnp.dot(inputs, up_ref[...], preferred_element_type=f32)
    hidden = (gate * (1.0 / (1.0 + jnp.exp(-gate))) * up).astype(bf16)
    send_rows(hidden, down_ref, order_ref, out_ref)


def mix_rows(returned_ref, hidden_ref, ids_ref, weights_ref, out_ref, natural):
    rows, width = hidden_ref.shape
    strips = width // strip
    base = lax.axis_index("ctx") * rows
    for row in range(rows):
        mixed = sum(
            weights_ref[k, base + row] * returned_ref[ids_ref[k, base + row]].astype(f32)
            for k in range(ids_ref.shape[0])
        )
        for part in range(strips):
            at = row * strips + part
            natural[row : row + 1, part * strip : (part + 1) * strip] = mixed[at : at + 1]
    out_ref[...] = (hidden_ref[...] + natural[0:rows, :]).astype(bf16)


def kernel_layer(
    query_latent,
    query_rope,
    cache_latent,
    cache_rope,
    valid_len,
    w_vo,
    residual,
    norm_gain,
    expert_ids,
    route_weight,
    w_gate,
    w_up,
    w_down,
):
    devices = lax.axis_size("ctx")
    rows, width = residual.shape
    block_len, latent = cache_latent.shape
    rope_dim = cache_rope.shape[0]
    head_count = query_rope.shape[1] // rope_dim
    total_rows = rows * devices
    heads_each = head_count // share
    groups = devices // share
    per = rows * heads_each
    strips = width // strip
    height = 8 * -(-rows * strips // 8)

    def swap(array, mask):
        return lax.ppermute(array, "ctx", [(d, d ^ mask) for d in range(devices)])

    own = jnp.concatenate([cache_latent, cache_rope], axis=0)
    near = swap(own, 2)
    core = swap(own, 1)
    tiles = 2 * per // 8 * 2 + 1
    outgoing = call(
        functools.partial(pack_queries, rows, heads_each, latent, rope_dim),
        jax.ShapeDtypeStruct((devices, tiles, 8, 128), bf16),
        query_latent,
        query_rope,
        scratch=[VMEM((share, 2 * per, latent // 2), f32), VMEM((share, 16, 128), f32)],
    )
    arrived = lax.all_to_all(outgoing, "ctx", split_axis=0, concat_axis=0, tiled=True)
    far = swap(near, 1)
    order, rope_order = query_order(rows, devices, heads_each, total_rows)
    partial = call(
        functools.partial(attend, rows, heads_each, block_len, latent),
        jax.ShapeDtypeStruct((heads_each, total_rows + 8, latent), bf16),
        arrived,
        order,
        rope_order,
        valid_len,
        own,
        core,
        near,
        far,
        spaces={3: SMEM},
        scratch=[VMEM((total_rows, 128), jnp.int32), VMEM((share, heads_each * total_rows, block_len), f32)],
    )
    lines = [[share * g + p for g in range(groups)] for p in range(share)]
    pieces = lax.all_to_all(partial, "ctx", split_axis=0, concat_axis=0, axis_index_groups=lines, tiled=True)
    send = strip_order(rows, devices, strips, height)
    send_order, back_order = jnp.asarray(send, bf16), jnp.asarray(send.T, bf16)
    strip_shape = jax.ShapeDtypeStruct((devices, height, strip), bf16)
    columns = call(
        merge_project, strip_shape, pieces, w_vo, send_order, scratch=[VMEM((total_rows, latent), f32)]
    )
    summed = lax.all_to_all(columns, "ctx", split_axis=0, concat_axis=0, tiled=True)
    attn_out, hidden_state, normed = call(
        norm_rows,
        (
            jax.ShapeDtypeStruct((rows, width), bf16),
            jax.ShapeDtypeStruct((rows, width), f32),
            strip_shape,
        ),
        summed,
        residual,
        norm_gain[None, :],
        scratch=[VMEM((8, width), f32), VMEM((height, strip), f32)],
    )
    inputs = lax.all_to_all(normed, "ctx", split_axis=0, concat_axis=0, tiled=True)
    result = call(run_expert, strip_shape, inputs, back_order, send_order, w_gate[0], w_up[0], w_down[0])
    returned = lax.all_to_all(result, "ctx", split_axis=0, concat_axis=0, tiled=True)
    layer_out = call(
        mix_rows,
        jax.ShapeDtypeStruct((rows, width), bf16),
        returned,
        hidden_state,
        expert_ids.T,
        route_weight.T,
        spaces={2: SMEM, 3: SMEM},
        scratch=[VMEM((8, width), f32)],
    )
    return attn_out, layer_out


def fits(mesh, query_rope, residual, cache_latent, cache_rope):
    devices = mesh.shape["ctx"]
    rope_dim = cache_rope.shape[0] // mesh.shape["groups"]
    heads = query_rope.shape[1] // rope_dim
    rows = residual.shape[0] // (devices * mesh.shape["groups"])
    per = rows * heads // share
    return (
        heads == devices
        and devices % share == 0
        and rope_dim == 64
        and 2 * per % 8 == 0
        and 8 <= per <= 16
        and rows * devices % 16 == 0
        and rows * devices <= 128
        and cache_latent.shape[1] == 512
        and residual.shape[1] % strip == 0
    )


def solution(mesh):
    in_specs = (
        P(("groups", "ctx"), None),
        P(("groups", "ctx"), None),
        P(("groups", "ctx"), None),
        P("groups", "ctx"),
        P("groups"),
        P("ctx", None),
        P(("groups", "ctx"), None),
        P(),
        P("groups", None),
        P("groups", None),
        P("ctx", None, None),
        P("ctx", None, None),
        P("ctx", None, None),
    )
    out_specs = (P(("groups", "ctx"), None), P(("groups", "ctx"), None))

    def layer(*args):
        body = kernel_layer if fits(mesh, args[1], args[6], args[2], args[3]) else plain_layer
        return jax.shard_map(body, mesh=mesh, in_specs=in_specs, out_specs=out_specs, check_vma=False)(*args)

    return layer
```

```python
import functools

import jax
import jax.numpy as jnp
import numpy as np
from jax import lax
from jax.experimental import pallas as pl
from jax.experimental.pallas import tpu as pltpu
from jax.sharding import PartitionSpec as P


softmax_scale = 192.0 ** (-0.5)
negative_fill = -1e30
norm_eps = 1e-06
share = 4
strip = 512

VMEM = pltpu.VMEM
SMEM = pltpu.SMEM
f32 = jnp.float32
bf16 = jnp.bfloat16


def expert_apply(inputs, gate_weight, up_weight, down_weight):
    gate_out = jnp.dot(inputs, gate_weight, preferred_element_type=jnp.float32)
    up_out = jnp.dot(inputs, up_weight, preferred_element_type=jnp.float32)
    hidden = (jax.nn.silu(gate_out) * up_out).astype(jnp.bfloat16)
    return jnp.dot(hidden, down_weight, preferred_element_type=jnp.float32).astype(jnp.bfloat16)


def plain_layer(
    query_latent,
    query_rope,
    cache_latent,
    cache_rope,
    valid_len,
    w_vo,
    residual,
    norm_gain,
    expert_ids,
    route_weight,
    w_gate,
    w_up,
    w_down,
):
    query_all, rope_all = (
        lax.all_gather(query_latent, "ctx", axis=0, tiled=True),
        lax.all_gather(query_rope, "ctx", axis=0, tiled=True),
    )
    total_rows = query_all.shape[0]
    own_rows = residual.shape[0]
    latent = cache_latent.shape[1]
    rope_dim = cache_rope.shape[0]
    head_count = rope_all.shape[1] // rope_dim
    block_len = cache_latent.shape[0]
    devices = lax.axis_size("ctx")
    self_index = lax.axis_index("ctx")
    col_count = head_count * latent // devices
    flat_query = query_all.reshape(total_rows * head_count, latent)
    flat_rope = rope_all.reshape(total_rows * head_count, rope_dim)
    scores = lax.dot_general(
        flat_query, cache_latent, (((1,), (1,)), ((), ())), preferred_element_type=jnp.float32
    )
    scores = (
        scores + jnp.dot(flat_rope, cache_rope, preferred_element_type=jnp.float32)
    ) * softmax_scale
    position = self_index * block_len + lax.broadcasted_iota(jnp.int32, (1, block_len), 1)
    usable = position < jnp.repeat(valid_len, head_count)[:, None]
    block_max = jnp.max(jnp.where(usable, scores, negative_fill), axis=1)
    weights = jnp.where(usable, jnp.exp(scores - block_max[:, None]), 0.0).astype(jnp.bfloat16)
    block_sum = jnp.sum(weights.astype(jnp.float32), axis=1)
    block_out = jnp.dot(weights, cache_latent, preferred_element_type=jnp.float32)
    row_max = block_max.reshape(total_rows, head_count)
    row_sum = block_sum.reshape(total_rows, head_count)
    global_max = lax.pmax(row_max, "ctx")
    factor = jnp.exp(row_max - global_max)
    scaled = (block_out.reshape(total_rows, head_count, latent) * factor[:, :, None]).reshape(
        total_rows, head_count * latent
    )
    merged = lax.psum_scatter(scaled, "ctx", scatter_dimension=1, tiled=True)
    totals = lax.psum(row_sum * factor, "ctx")
    divisor = lax.dynamic_slice_in_dim(totals, self_index * col_count // latent, 1, 1)
    attention = (merged / divisor).astype(jnp.bfloat16)
    projected = lax.psum_scatter(
        jnp.dot(attention, w_vo, preferred_element_type=jnp.float32),
        "ctx",
        scatter_dimension=0,
        tiled=True,
    )
    hidden_state = residual.astype(jnp.float32) + projected
    normed = (
        hidden_state
        * lax.rsqrt(jnp.mean(hidden_state * hidden_state, axis=1, keepdims=True) + norm_eps)
        * norm_gain
    ).astype(jnp.bfloat16)
    expert_iota = lax.broadcasted_iota(jnp.int32, (1, 1, devices), 2)
    route_table = jnp.sum(
        jnp.where(expert_ids[:, :, None] == expert_iota, route_weight[:, :, None], 0.0), axis=1
    )
    gate_own = w_gate[0]
    up_own = w_up[0]
    down_own = w_down[0]
    own_table = jnp.transpose(
        lax.dynamic_slice_in_dim(route_table, self_index * own_rows, own_rows, 0)
    )
    outgoing = jnp.where(
        own_table[:, :, None] > 0.0, normed[None, :, :], jnp.zeros((), jnp.bfloat16)
    )
    arrived = lax.all_to_all(outgoing, "ctx", split_axis=0, concat_axis=0, tiled=True)
    item_count = arrived.shape[1]
    stacked = arrived.reshape(devices * item_count, arrived.shape[2])
    result = expert_apply(stacked, gate_own, up_own, down_own).reshape(
        devices, item_count, arrived.shape[2]
    )
    returned = lax.all_to_all(result, "ctx", split_axis=0, concat_axis=0, tiled=True)
    mixture = jnp.sum(own_table[:, :, None] * returned.astype(jnp.float32), axis=0)
    layer_out = (hidden_state + mixture).astype(jnp.bfloat16)
    return (projected.astype(jnp.bfloat16), layer_out)


def call(kernel, out_shape, *operands, spaces=None, scratch=(), limit=24):
    spaces = spaces or {}
    in_specs = [pl.BlockSpec(memory_space=spaces.get(i, VMEM)) for i in range(len(operands))]
    many = isinstance(out_shape, (tuple, list))
    out_specs = [pl.BlockSpec(memory_space=VMEM) for _ in out_shape] if many else pl.BlockSpec(memory_space=VMEM)
    return pl.pallas_call(
        kernel,
        out_shape=out_shape,
        in_specs=in_specs,
        out_specs=out_specs,
        scratch_shapes=list(scratch),
        compiler_params=pltpu.CompilerParams(vmem_limit_bytes=limit << 20),
        cost_estimate=pl.CostEstimate(flops=4 * 10**9, bytes_accessed=64 << 20, transcendentals=0),
    )(*operands)


def strip_order(rows, devices, strips, height):
    order = np.zeros((devices * height, strips * rows * devices), np.float32)
    for device in range(devices):
        for row in range(rows):
            for part in range(strips):
                order[device * height + row * strips + part, part * rows * devices + device * rows + row] = 1.0
    return order


def prepare(heads_each, query_hbm, rope_hbm, latent_hbm, keys_hbm, out_ref, own_ref, query_ref, rope_ref, piece, rope_piece, arrive):
    block_len, latent = latent_hbm.shape
    copies = [
        pltpu.make_async_copy(query_hbm, query_ref, arrive.at[0]),
        pltpu.make_async_copy(rope_hbm, rope_ref, arrive.at[1]),
        pltpu.make_async_copy(latent_hbm, own_ref.at[0:block_len], arrive.at[2]),
        pltpu.make_async_copy(keys_hbm, own_ref.at[block_len:], arrive.at[3]),
    ]
    for copy in copies:
        copy.start()
    rows = query_ref.shape[0]
    per = rows * heads_each
    rope_dim = rope_ref.shape[1] // (heads_each * share)
    half_width = latent // 2
    groups = out_ref.shape[0] // share
    lane = lax.broadcasted_iota(jnp.int32, (8, 128), 1)
    rope_piece[...] = jnp.zeros_like(rope_piece)
    copies[0].wait()
    copies[1].wait()
    query = query_ref[...].astype(f32)
    rope = rope_ref[...].astype(f32)
    for place in range(share):
        for item in range(per):
            row, index = divmod(item, heads_each)
            head = share * index + place
            for half in range(2):
                begin = head * latent + half * half_width
                piece[place, half * per + item : half * per + item + 1, :] = query[row : row + 1, begin : begin + half_width]
            block = head * rope_dim // 128
            rope_piece[place, item : item + 1, :] = rope[row : row + 1, block * 128 : (block + 1) * 128]
    for place in range(share):
        first = rope_piece[place, 0:8, :]
        second = rope_piece[place, 8:16, :]
        if place % 2 == 1:
            first = pltpu.roll(first, 64, 1)
        else:
            second = pltpu.roll(second, 64, 1)
        tail = jnp.where(lane < 64, first, second).astype(bf16)
        tiles = []
        for rt in range(2 * per // 8):
            for lt in range(half_width // 128):
                tiles.append(piece[place, rt * 8 : (rt + 1) * 8, lt * 128 : (lt + 1) * 128].astype(bf16))
        tiles.append(tail)
        for group in range(groups):
            for index, tile in enumerate(tiles):
                out_ref[group * share + place, index] = tile
    copies[2].wait()
    copies[3].wait()


def place_of(item, source, rows, heads_each, total_rows):
    row = sum((item >= step * heads_each).astype(jnp.int32) for step in range(1, rows))
    head = item - row * heads_each
    return head * total_rows + source * rows + row


def one_hot(target, height):
    return (lax.broadcasted_iota(jnp.int32, (height, target.shape[1]), 0) == target).astype(f32).astype(bf16)


def score_block(query, rope_query, keys, rope_keys, begin, limits, heads_each):
    flat, latent = query.shape
    total_rows = flat // heads_each
    block_len = rope_keys.shape[1]
    empty = jnp.zeros_like(rope_keys)
    rope_keys = jnp.concatenate([rope_keys, empty, empty, rope_keys], axis=0)
    scores = lax.dot_general(query, keys, (((1,), (1,)), ((), ())), preferred_element_type=f32)
    scores = (scores + jnp.dot(rope_query, rope_keys, preferred_element_type=f32)) * softmax_scale
    valid = lax.broadcasted_iota(jnp.int32, (total_rows, block_len), 1) + begin < limits
    return jnp.where(valid[None], scores.reshape(heads_each, total_rows, block_len), negative_fill).reshape(flat, block_len)


def score_near(rows, heads_each, arrived_ref, length_ref, own_ref, own_rope_ref, core_ref, query_ref, rope_query_ref, scores_ref, limit_ref):
    devices = arrived_ref.shape[0]
    total_rows = rows * devices
    flat = heads_each * total_rows
    per = rows * heads_each
    row_tiles = 2 * per // 8
    block_len, latent = own_ref.shape
    me = lax.axis_index("ctx")
    for row in range(total_rows):
        limit_ref[row : row + 1, :] = jnp.full((1, 128), length_ref[row], jnp.int32)
    column = lax.broadcasted_iota(jnp.int32, (1, row_tiles * devices * 8), 1)
    source = lax.rem(lax.shift_right_logical(column, 3), devices)
    unit = lax.div(column, devices * 8) * 8 + lax.rem(column, 8)
    second = (unit >= per).astype(jnp.int32)
    target = second * flat + place_of(unit - second * per, source, rows, heads_each, total_rows)
    gathered = jnp.concatenate(
        [
            jnp.concatenate(
                [arrived_ref[:, 2 * rt + lt].reshape(devices * 8, 128) for lt in range(2)], axis=1
            )
            for rt in range(row_tiles)
        ],
        axis=0,
    )
    ordered = jnp.dot(one_hot(target, 2 * flat), gathered, preferred_element_type=f32).astype(bf16)
    query = jnp.concatenate([ordered[:flat], ordered[flat:]], axis=1)
    column = lax.broadcasted_iota(jnp.int32, (1, devices * 8), 1)
    source = lax.shift_right_logical(column, 3)
    item = lax.rem(column, 8)
    rope_rows = arrived_ref[:, 2 * row_tiles].reshape(devices * 8, 128)
    halves = []
    for half in range(2):
        shifted = item + 8 * half
        target = jnp.where(shifted < per, place_of(shifted, source, rows, heads_each, total_rows), -1)
        halves.append(jnp.dot(one_hot(target, flat), rope_rows, preferred_element_type=f32).astype(bf16))
    rope_query = jnp.concatenate(halves, axis=1)
    query_ref[...] = query
    rope_query_ref[...] = rope_query
    limits = limit_ref[...][:, 0:1]
    blocks = ((own_ref[...], own_rope_ref[...]), (core_ref[0:latent, :], core_ref[latent:, :]))
    for index, (keys, rope_keys) in enumerate(blocks):
        begin = lax.bitwise_xor(me, index) * block_len
        scores_ref[index] = score_block(query, rope_query, keys, rope_keys, begin, limits, heads_each)


def attend(heads_each, query_ref, rope_query_ref, scores_ref, limit_ref, own_ref, core_ref, near_ref, far_ref, out_ref, more_ref):
    flat, latent = query_ref.shape
    total_rows = flat // heads_each
    block_len = own_ref.shape[0]
    me = lax.axis_index("ctx")
    limits = limit_ref[...][:, 0:1]
    query, rope_query = query_ref[...], rope_query_ref[...]
    highest = jnp.maximum(
        jnp.max(scores_ref[0], axis=1, keepdims=True), jnp.max(scores_ref[1], axis=1, keepdims=True)
    )
    for index, block in enumerate((near_ref, far_ref)):
        begin = lax.bitwise_xor(me, index + 2) * block_len
        scores = score_block(query, rope_query, block[0:latent, :], block[latent:, :], begin, limits, heads_each)
        more_ref[index] = scores
        highest = jnp.maximum(highest, jnp.max(scores, axis=1, keepdims=True))
    total = None
    summed = None
    for index, block in enumerate((own_ref, core_ref, near_ref, far_ref)):
        begin = lax.bitwise_xor(me, index) * block_len
        valid = lax.broadcasted_iota(jnp.int32, (total_rows, block_len), 1) + begin < limits
        scores = scores_ref[index] if index < 2 else more_ref[index - 2]
        weights = jnp.exp(scores - highest)
        weights = jnp.where(valid[None], weights.reshape(heads_each, total_rows, block_len), 0.0).reshape(flat, block_len)
        weights = weights.astype(bf16)
        part = jnp.sum(weights.astype(f32), axis=1, keepdims=True)
        summed = part if summed is None else summed + part
        part = jnp.dot(weights, block[0:latent, :], preferred_element_type=f32)
        total = part if total is None else total + part
    lane = lax.broadcasted_iota(jnp.int32, (8, 128), 1)
    for head in range(heads_each):
        base = head * total_rows
        out_ref[head, 0:total_rows, :] = total[base : base + total_rows].astype(bf16)
        note = jnp.zeros((8, 128), f32)
        for tile in range(total_rows // 8):
            for offset, value in ((0, highest), (3, summed)):
                value = jnp.broadcast_to(value[base + tile * 8 : base + tile * 8 + 8], (8, 128))
                for piece in range(3):
                    rounded = value.astype(bf16).astype(f32)
                    note = jnp.where(lane == 8 * tile + offset + piece, rounded, note)
                    value = value - rounded
        wide = jnp.concatenate([note, jnp.zeros((8, out_ref.shape[2] - 128), f32)], axis=1)
        out_ref[head, total_rows:, :] = wide.astype(bf16)


def merge_project(arrived_ref, weight_ref, order_ref, out_ref, attention_ref):
    sources, height, latent = arrived_ref.shape
    total_rows = height - 8
    peaks = []
    sums = []
    for source in range(sources):
        note = arrived_ref[source, total_rows:, 0:128].astype(f32)
        shifted = [note] + [pltpu.roll(note, 128 - step, 1) for step in range(1, 6)]
        peaks.append(shifted[0] + shifted[1] + shifted[2])
        sums.append(shifted[3] + shifted[4] + shifted[5])
    highest = functools.reduce(jnp.maximum, peaks)
    factors = [jnp.exp(peak - highest) for peak in peaks]
    divisor = sum(factor * part for factor, part in zip(factors, sums))
    factors = [factor / divisor for factor in factors]
    for tile in range(total_rows // 8):
        span = slice(tile * 8, tile * 8 + 8)
        attention_ref[span, :] = sum(
            factor[:, 8 * tile : 8 * tile + 1] * arrived_ref[source, span, :].astype(f32)
            for source, factor in enumerate(factors)
        )
    attention = attention_ref[...].astype(bf16)
    send_rows(attention, weight_ref, order_ref, out_ref)


def send_rows(left, weight_ref, order_ref, out_ref):
    strips = weight_ref.shape[1] // strip
    parts = [
        jnp.dot(left, weight_ref[:, part * strip : (part + 1) * strip], preferred_element_type=f32).astype(bf16)
        for part in range(strips)
    ]
    stacked = jnp.concatenate(parts, axis=0)
    ordered = jnp.dot(order_ref[...], stacked, preferred_element_type=f32).astype(bf16)
    out_ref[...] = ordered.reshape(out_ref.shape)


def norm_rows(arrived_ref, residual_ref, gain_ref, attn_ref, hidden_ref, out_ref, natural, stripped):
    rows, width = residual_ref.shape
    strips = width // strip
    summed = jnp.sum(arrived_ref[...].astype(f32), axis=0)
    for row in range(rows):
        for part in range(strips):
            at = row * strips + part
            natural[row : row + 1, part * strip : (part + 1) * strip] = summed[at : at + 1]
    projected = natural[0:rows, :]
    attn_ref[...] = projected.astype(bf16)
    hidden = residual_ref[...].astype(f32) + projected
    hidden_ref[...] = hidden
    normed = hidden * lax.rsqrt(jnp.mean(hidden * hidden, axis=1, keepdims=True) + norm_eps) * gain_ref[...].reshape(1, width)
    stripped[...] = jnp.zeros_like(stripped)
    for row in range(rows):
        for part in range(strips):
            at = row * strips + part
            stripped[at : at + 1, :] = normed[row : row + 1, part * strip : (part + 1) * strip]
    tile = stripped[...].astype(bf16)
    for device in range(out_ref.shape[0]):
        out_ref[device] = tile


def run_expert(arrived_ref, back_ref, order_ref, gate_ref, up_ref, down_ref, out_ref):
    devices, height, _ = arrived_ref.shape
    strips = gate_ref.shape[0] // strip
    pieces = arrived_ref[...].reshape(devices * height, strip)
    ordered = jnp.dot(back_ref[...], pieces, preferred_element_type=f32).astype(bf16)
    total_rows = ordered.shape[0] // strips
    inputs = jnp.concatenate([ordered[part * total_rows : (part + 1) * total_rows] for part in range(strips)], axis=1)
    gate = jnp.dot(inputs, gate_ref[...], preferred_element_type=f32)
    up = jnp.dot(inputs, up_ref[...], preferred_element_type=f32)
    hidden = (gate * (1.0 / (1.0 + jnp.exp(-gate))) * up).astype(bf16)
    send_rows(hidden, down_ref, order_ref, out_ref)


def mix_rows(returned_ref, hidden_ref, ids_ref, weights_ref, out_ref, natural):
    rows, width = hidden_ref.shape
    strips = width // strip
    base = lax.axis_index("ctx") * rows
    for row in range(rows):
        mixed = sum(
            weights_ref[k, base + row] * returned_ref[ids_ref[k, base + row]].astype(f32)
            for k in range(ids_ref.shape[0])
        )
        for part in range(strips):
            at = row * strips + part
            natural[row : row + 1, part * strip : (part + 1) * strip] = mixed[at : at + 1]
    out_ref[...] = (hidden_ref[...] + natural[0:rows, :]).astype(bf16)


def kernel_layer(
    query_latent,
    query_rope,
    cache_latent,
    cache_rope,
    valid_len,
    w_vo,
    residual,
    norm_gain,
    expert_ids,
    route_weight,
    w_gate,
    w_up,
    w_down,
):
    devices = lax.axis_size("ctx")
    rows, width = residual.shape
    block_len, latent = cache_latent.shape
    rope_dim = cache_rope.shape[0]
    head_count = query_rope.shape[1] // rope_dim
    total_rows = rows * devices
    heads_each = head_count // share
    groups = devices // share
    per = rows * heads_each
    strips = width // strip
    height = 8 * -(-rows * strips // 8)

    def swap(array, mask):
        return lax.ppermute(array, "ctx", [(d, d ^ mask) for d in range(devices)])

    tiles = 2 * per // 8 * 2 + 1
    flat = heads_each * total_rows
    outgoing, own = call(
        functools.partial(prepare, heads_each),
        (
            jax.ShapeDtypeStruct((devices, tiles, 8, 128), bf16),
            jax.ShapeDtypeStruct((latent + rope_dim, block_len), bf16),
        ),
        query_latent,
        query_rope,
        cache_latent,
        cache_rope,
        spaces={i: pltpu.HBM for i in range(4)},
        limit=60,
        scratch=[
            VMEM(query_latent.shape, bf16),
            VMEM(query_rope.shape, bf16),
            VMEM((share, 2 * per, latent // 2), f32),
            VMEM((share, 16, 128), f32),
            pltpu.SemaphoreType.DMA((4,)),
        ],
    )
    near = swap(own, 2)
    core = swap(own, 1)
    arrived = lax.all_to_all(outgoing, "ctx", split_axis=0, concat_axis=0, tiled=True)
    near, arrived = lax.optimization_barrier((near, arrived))
    far = swap(near, 1)
    query, rope_query, scores, limits = call(
        functools.partial(score_near, rows, heads_each),
        (
            jax.ShapeDtypeStruct((flat, latent), bf16),
            jax.ShapeDtypeStruct((flat, 256), bf16),
            jax.ShapeDtypeStruct((2, flat, block_len), f32),
            jax.ShapeDtypeStruct((total_rows, 128), jnp.int32),
        ),
        arrived,
        valid_len,
        cache_latent,
        cache_rope,
        core,
        spaces={1: SMEM},
    )
    partial = call(
        functools.partial(attend, heads_each),
        jax.ShapeDtypeStruct((heads_each, total_rows + 8, latent), bf16),
        query,
        rope_query,
        scores,
        limits,
        cache_latent,
        core,
        near,
        far,
        scratch=[VMEM((2, flat, block_len), f32)],
    )
    lines = [[share * g + p for g in range(groups)] for p in range(share)]
    pieces = lax.all_to_all(partial, "ctx", split_axis=0, concat_axis=0, axis_index_groups=lines, tiled=True)
    send = strip_order(rows, devices, strips, height)
    send_order, back_order = jnp.asarray(send, bf16), jnp.asarray(send.T, bf16)
    strip_shape = jax.ShapeDtypeStruct((devices, height, strip), bf16)
    columns = call(
        merge_project, strip_shape, pieces, w_vo, send_order, scratch=[VMEM((total_rows, latent), f32)]
    )
    summed = lax.all_to_all(columns, "ctx", split_axis=0, concat_axis=0, tiled=True)
    attn_out, hidden_state, normed = call(
        norm_rows,
        (
            jax.ShapeDtypeStruct((rows, width), bf16),
            jax.ShapeDtypeStruct((rows, width), f32),
            strip_shape,
        ),
        summed,
        residual,
        norm_gain,
        scratch=[VMEM((8, width), f32), VMEM((height, strip), f32)],
    )
    inputs = lax.all_to_all(normed, "ctx", split_axis=0, concat_axis=0, tiled=True)
    result = call(run_expert, strip_shape, inputs, back_order, send_order, w_gate[0], w_up[0], w_down[0])
    returned = lax.all_to_all(result, "ctx", split_axis=0, concat_axis=0, tiled=True)
    layer_out = call(
        mix_rows,
        jax.ShapeDtypeStruct((rows, width), bf16),
        returned,
        hidden_state,
        expert_ids.T,
        route_weight.T,
        spaces={2: SMEM, 3: SMEM},
        scratch=[VMEM((8, width), f32)],
    )
    return attn_out, layer_out


def fits(mesh, query_rope, residual, cache_latent, cache_rope):
    devices = mesh.shape["ctx"]
    rope_dim = cache_rope.shape[0] // mesh.shape["groups"]
    heads = query_rope.shape[1] // rope_dim
    rows = residual.shape[0] // (devices * mesh.shape["groups"])
    per = rows * heads // share
    return (
        heads == devices
        and devices % share == 0
        and rope_dim == 64
        and 2 * per % 8 == 0
        and 8 <= per <= 16
        and rows * devices % 16 == 0
        and rows * devices <= 128
        and cache_latent.shape[1] == 512
        and cache_latent.shape[0] // (devices * mesh.shape["groups"]) == 512
        and devices & (devices - 1) == 0
        and residual.shape[1] % strip == 0
    )


def solution(mesh):
    in_specs = (
        P(("groups", "ctx"), None),
        P(("groups", "ctx"), None),
        P(("groups", "ctx"), None),
        P("groups", "ctx"),
        P("groups"),
        P("ctx", None),
        P(("groups", "ctx"), None),
        P(),
        P("groups", None),
        P("groups", None),
        P("ctx", None, None),
        P("ctx", None, None),
        P("ctx", None, None),
    )
    out_specs = (P(("groups", "ctx"), None), P(("groups", "ctx"), None))

    def layer(*args):
        body = kernel_layer if fits(mesh, args[1], args[6], args[2], args[3]) else plain_layer
        return jax.shard_map(body, mesh=mesh, in_specs=in_specs, out_specs=out_specs, check_vma=False)(*args)

    return layer
```

```python
import functools

import jax
import jax.numpy as jnp
import numpy as np
from jax import lax
from jax.experimental import pallas as pl
from jax.experimental.pallas import tpu as pltpu
from jax.sharding import PartitionSpec as P


softmax_scale = 192.0 ** (-0.5)
negative_fill = -1e30
norm_eps = 1e-06
share = 4
strip = 512

VMEM = pltpu.VMEM
SMEM = pltpu.SMEM
f32 = jnp.float32
bf16 = jnp.bfloat16


def expert_apply(inputs, gate_weight, up_weight, down_weight):
    gate_out = jnp.dot(inputs, gate_weight, preferred_element_type=jnp.float32)
    up_out = jnp.dot(inputs, up_weight, preferred_element_type=jnp.float32)
    hidden = (jax.nn.silu(gate_out) * up_out).astype(jnp.bfloat16)
    return jnp.dot(hidden, down_weight, preferred_element_type=jnp.float32).astype(jnp.bfloat16)


def plain_layer(
    query_latent,
    query_rope,
    cache_latent,
    cache_rope,
    valid_len,
    w_vo,
    residual,
    norm_gain,
    expert_ids,
    route_weight,
    w_gate,
    w_up,
    w_down,
):
    query_all, rope_all = (
        lax.all_gather(query_latent, "ctx", axis=0, tiled=True),
        lax.all_gather(query_rope, "ctx", axis=0, tiled=True),
    )
    total_rows = query_all.shape[0]
    own_rows = residual.shape[0]
    latent = cache_latent.shape[1]
    rope_dim = cache_rope.shape[0]
    head_count = rope_all.shape[1] // rope_dim
    block_len = cache_latent.shape[0]
    devices = lax.axis_size("ctx")
    self_index = lax.axis_index("ctx")
    col_count = head_count * latent // devices
    flat_query = query_all.reshape(total_rows * head_count, latent)
    flat_rope = rope_all.reshape(total_rows * head_count, rope_dim)
    scores = lax.dot_general(
        flat_query, cache_latent, (((1,), (1,)), ((), ())), preferred_element_type=jnp.float32
    )
    scores = (
        scores + jnp.dot(flat_rope, cache_rope, preferred_element_type=jnp.float32)
    ) * softmax_scale
    position = self_index * block_len + lax.broadcasted_iota(jnp.int32, (1, block_len), 1)
    usable = position < jnp.repeat(valid_len, head_count)[:, None]
    block_max = jnp.max(jnp.where(usable, scores, negative_fill), axis=1)
    weights = jnp.where(usable, jnp.exp(scores - block_max[:, None]), 0.0).astype(jnp.bfloat16)
    block_sum = jnp.sum(weights.astype(jnp.float32), axis=1)
    block_out = jnp.dot(weights, cache_latent, preferred_element_type=jnp.float32)
    row_max = block_max.reshape(total_rows, head_count)
    row_sum = block_sum.reshape(total_rows, head_count)
    global_max = lax.pmax(row_max, "ctx")
    factor = jnp.exp(row_max - global_max)
    scaled = (block_out.reshape(total_rows, head_count, latent) * factor[:, :, None]).reshape(
        total_rows, head_count * latent
    )
    merged = lax.psum_scatter(scaled, "ctx", scatter_dimension=1, tiled=True)
    totals = lax.psum(row_sum * factor, "ctx")
    divisor = lax.dynamic_slice_in_dim(totals, self_index * col_count // latent, 1, 1)
    attention = (merged / divisor).astype(jnp.bfloat16)
    projected = lax.psum_scatter(
        jnp.dot(attention, w_vo, preferred_element_type=jnp.float32),
        "ctx",
        scatter_dimension=0,
        tiled=True,
    )
    hidden_state = residual.astype(jnp.float32) + projected
    normed = (
        hidden_state
        * lax.rsqrt(jnp.mean(hidden_state * hidden_state, axis=1, keepdims=True) + norm_eps)
        * norm_gain
    ).astype(jnp.bfloat16)
    expert_iota = lax.broadcasted_iota(jnp.int32, (1, 1, devices), 2)
    route_table = jnp.sum(
        jnp.where(expert_ids[:, :, None] == expert_iota, route_weight[:, :, None], 0.0), axis=1
    )
    gate_own = w_gate[0]
    up_own = w_up[0]
    down_own = w_down[0]
    own_table = jnp.transpose(
        lax.dynamic_slice_in_dim(route_table, self_index * own_rows, own_rows, 0)
    )
    outgoing = jnp.where(
        own_table[:, :, None] > 0.0, normed[None, :, :], jnp.zeros((), jnp.bfloat16)
    )
    arrived = lax.all_to_all(outgoing, "ctx", split_axis=0, concat_axis=0, tiled=True)
    item_count = arrived.shape[1]
    stacked = arrived.reshape(devices * item_count, arrived.shape[2])
    result = expert_apply(stacked, gate_own, up_own, down_own).reshape(
        devices, item_count, arrived.shape[2]
    )
    returned = lax.all_to_all(result, "ctx", split_axis=0, concat_axis=0, tiled=True)
    mixture = jnp.sum(own_table[:, :, None] * returned.astype(jnp.float32), axis=0)
    layer_out = (hidden_state + mixture).astype(jnp.bfloat16)
    return (projected.astype(jnp.bfloat16), layer_out)


def call(kernel, out_shape, *operands, spaces=None, scratch=(), limit=24):
    spaces = spaces or {}
    in_specs = [pl.BlockSpec(memory_space=spaces.get(i, VMEM)) for i in range(len(operands))]
    many = isinstance(out_shape, (tuple, list))
    out_specs = [pl.BlockSpec(memory_space=VMEM) for _ in out_shape] if many else pl.BlockSpec(memory_space=VMEM)
    return pl.pallas_call(
        kernel,
        out_shape=out_shape,
        in_specs=in_specs,
        out_specs=out_specs,
        scratch_shapes=list(scratch),
        compiler_params=pltpu.CompilerParams(vmem_limit_bytes=limit << 20),
        cost_estimate=pl.CostEstimate(flops=4 * 10**9, bytes_accessed=64 << 20, transcendentals=0),
    )(*operands)


def strip_order(rows, devices, strips, height):
    order = np.zeros((devices * height, strips * rows * devices), np.float32)
    for device in range(devices):
        for row in range(rows):
            for part in range(strips):
                order[device * height + row * strips + part, part * rows * devices + device * rows + row] = 1.0
    return order


def prepare(heads_each, query_ref, rope_ref, out_ref, piece, rope_piece):
    rows = query_ref.shape[0]
    per = rows * heads_each
    latent = query_ref.shape[1] // (heads_each * share)
    rope_dim = rope_ref.shape[1] // (heads_each * share)
    half_width = latent // 2
    groups = out_ref.shape[0] // share
    lane = lax.broadcasted_iota(jnp.int32, (8, 128), 1)
    rope_piece[...] = jnp.zeros_like(rope_piece)
    query = query_ref[...].astype(f32)
    rope = rope_ref[...].astype(f32)
    for place in range(share):
        for item in range(per):
            row, index = divmod(item, heads_each)
            head = share * index + place
            for half in range(2):
                begin = head * latent + half * half_width
                piece[place, half * per + item : half * per + item + 1, :] = query[row : row + 1, begin : begin + half_width]
            block = head * rope_dim // 128
            rope_piece[place, item : item + 1, :] = rope[row : row + 1, block * 128 : (block + 1) * 128]
    for place in range(share):
        first = rope_piece[place, 0:8, :]
        second = rope_piece[place, 8:16, :]
        if place % 2 == 1:
            first = pltpu.roll(first, 64, 1)
        else:
            second = pltpu.roll(second, 64, 1)
        tail = jnp.where(lane < 64, first, second).astype(bf16)
        tiles = []
        for rt in range(2 * per // 8):
            for lt in range(half_width // 128):
                tiles.append(piece[place, rt * 8 : (rt + 1) * 8, lt * 128 : (lt + 1) * 128].astype(bf16))
        tiles.append(tail)
        for group in range(groups):
            for index, tile in enumerate(tiles):
                out_ref[group * share + place, index] = tile


def place_of(item, source, rows, heads_each, total_rows):
    row = sum((item >= step * heads_each).astype(jnp.int32) for step in range(1, rows))
    head = item - row * heads_each
    core, chip = lax.rem(source, 2), lax.shift_right_logical(source, 1)
    return head * total_rows + core * (total_rows // 2) + chip * rows + row


def one_hot(target, height):
    return (lax.broadcasted_iota(jnp.int32, (height, target.shape[1]), 0) == target).astype(f32).astype(bf16)


def score_block(query, rope_query, keys, rope_keys, begin, limits, heads_each):
    flat, latent = query.shape
    total_rows = flat // heads_each
    block_len = rope_keys.shape[1]
    empty = jnp.zeros_like(rope_keys)
    rope_keys = jnp.concatenate([rope_keys, empty, empty, rope_keys], axis=0)
    scores = lax.dot_general(query, keys, (((1,), (1,)), ((), ())), preferred_element_type=f32)
    scores = (scores + jnp.dot(rope_query, rope_keys, preferred_element_type=f32)) * softmax_scale
    valid = lax.broadcasted_iota(jnp.int32, (total_rows, block_len), 1) + begin < limits
    return jnp.where(valid[None], scores.reshape(heads_each, total_rows, block_len), negative_fill).reshape(flat, block_len)


def score_near(rows, heads_each, arrived_ref, length_ref, own_ref, own_rope_ref, core_ref, core_rope_ref, query_ref, rope_query_ref, scores_ref, limit_ref):
    devices = arrived_ref.shape[0]
    total_rows = rows * devices
    flat = heads_each * total_rows
    per = rows * heads_each
    row_tiles = 2 * per // 8
    block_len, latent = own_ref.shape
    me = lax.axis_index("ctx")
    for row in range(total_rows):
        device, index = divmod(row, rows)
        at = device % 2 * (total_rows // 2) + device // 2 * rows + index
        limit_ref[at : at + 1, :] = jnp.full((1, 128), length_ref[row], jnp.int32)
    column = lax.broadcasted_iota(jnp.int32, (1, row_tiles * devices * 8), 1)
    source = lax.rem(lax.shift_right_logical(column, 3), devices)
    unit = lax.div(column, devices * 8) * 8 + lax.rem(column, 8)
    second = (unit >= per).astype(jnp.int32)
    target = second * flat + place_of(unit - second * per, source, rows, heads_each, total_rows)
    gathered = jnp.concatenate(
        [
            jnp.concatenate(
                [arrived_ref[:, 2 * rt + lt].reshape(devices * 8, 128) for lt in range(2)], axis=1
            )
            for rt in range(row_tiles)
        ],
        axis=0,
    )
    ordered = jnp.dot(one_hot(target, 2 * flat), gathered, preferred_element_type=f32).astype(bf16)
    query = jnp.concatenate([ordered[:flat], ordered[flat:]], axis=1)
    column = lax.broadcasted_iota(jnp.int32, (1, devices * 8), 1)
    source = lax.shift_right_logical(column, 3)
    item = lax.rem(column, 8)
    rope_rows = arrived_ref[:, 2 * row_tiles].reshape(devices * 8, 128)
    halves = []
    for half in range(2):
        shifted = item + 8 * half
        target = jnp.where(shifted < per, place_of(shifted, source, rows, heads_each, total_rows), -1)
        halves.append(jnp.dot(one_hot(target, flat), rope_rows, preferred_element_type=f32).astype(bf16))
    rope_query = jnp.concatenate(halves, axis=1)
    query_ref[...] = query
    rope_query_ref[...] = rope_query
    limits = limit_ref[...][:, 0:1]
    blocks = ((own_ref[...], own_rope_ref[...]), (core_ref[...], core_rope_ref[...]))
    for index, (keys, rope_keys) in enumerate(blocks):
        begin = lax.bitwise_xor(me, index) * block_len
        scores_ref[index] = score_block(query, rope_query, keys, rope_keys, begin, limits, heads_each)


def attend(heads_each, query_ref, rope_query_ref, scores_ref, limit_ref, own_ref, core_ref, near_ref, far_ref, near_rope_ref, far_rope_ref, out_ref, more_ref):
    flat, latent = query_ref.shape
    total_rows = flat // heads_each
    block_len = own_ref.shape[0]
    me = lax.axis_index("ctx")
    limits = limit_ref[...][:, 0:1]
    query, rope_query = query_ref[...], rope_query_ref[...]
    highest = jnp.maximum(
        jnp.max(scores_ref[0], axis=1, keepdims=True), jnp.max(scores_ref[1], axis=1, keepdims=True)
    )
    for index, (block, rope_block) in enumerate(((near_ref, near_rope_ref), (far_ref, far_rope_ref))):
        begin = lax.bitwise_xor(me, index + 2) * block_len
        scores = score_block(query, rope_query, block[...], rope_block[...], begin, limits, heads_each)
        more_ref[index] = scores
        highest = jnp.maximum(highest, jnp.max(scores, axis=1, keepdims=True))
    total = None
    summed = None
    for index, block in enumerate((own_ref, core_ref, near_ref, far_ref)):
        begin = lax.bitwise_xor(me, index) * block_len
        valid = lax.broadcasted_iota(jnp.int32, (total_rows, block_len), 1) + begin < limits
        scores = scores_ref[index] if index < 2 else more_ref[index - 2]
        weights = jnp.exp(scores - highest)
        weights = jnp.where(valid[None], weights.reshape(heads_each, total_rows, block_len), 0.0).reshape(flat, block_len)
        weights = weights.astype(bf16)
        part = jnp.sum(weights.astype(f32), axis=1, keepdims=True)
        summed = part if summed is None else summed + part
        part = jnp.dot(weights, block[...], preferred_element_type=f32)
        total = part if total is None else total + part
    lane = lax.broadcasted_iota(jnp.int32, (8, 128), 1)
    for head in range(heads_each):
        base = head * total_rows
        out_ref[head, 0:total_rows, :] = total[base : base + total_rows].astype(bf16)
        note = jnp.zeros((8, 128), f32)
        for tile in range(total_rows // 8):
            for offset, value in ((0, highest), (3, summed)):
                value = jnp.broadcast_to(value[base + tile * 8 : base + tile * 8 + 8], (8, 128))
                for piece in range(3):
                    rounded = value.astype(bf16).astype(f32)
                    note = jnp.where(lane == 8 * tile + offset + piece, rounded, note)
                    value = value - rounded
        wide = jnp.concatenate([note, jnp.zeros((8, out_ref.shape[2] - 128), f32)], axis=1)
        out_ref[head, total_rows:, :] = wide.astype(bf16)


def merge_project(arrived_ref, weight_ref, own_ref, other_ref, attention_ref, product_ref):
    sources, height, latent = arrived_ref.shape
    total_rows = height - 8
    peaks = []
    sums = []
    for source in range(sources):
        note = arrived_ref[source, total_rows:, 0:128].astype(f32)
        shifted = [note] + [pltpu.roll(note, 128 - step, 1) for step in range(1, 6)]
        peaks.append(shifted[0] + shifted[1] + shifted[2])
        sums.append(shifted[3] + shifted[4] + shifted[5])
    highest = functools.reduce(jnp.maximum, peaks)
    factors = [jnp.exp(peak - highest) for peak in peaks]
    divisor = sum(factor * part for factor, part in zip(factors, sums))
    factors = [factor / divisor for factor in factors]
    for tile in range(total_rows // 8):
        span = slice(tile * 8, tile * 8 + 8)
        attention_ref[span, :] = sum(
            factor[:, 8 * tile : 8 * tile + 1] * arrived_ref[source, span, :].astype(f32)
            for source, factor in enumerate(factors)
        )
    product = jnp.dot(attention_ref[...].astype(bf16), weight_ref[...], preferred_element_type=f32)
    product_ref[...] = product.reshape(product_ref.shape)
    core = lax.rem(lax.axis_index("ctx"), 2)
    own_ref[...] = product_ref[core]
    other_ref[...] = product_ref[1 - core].astype(bf16)


def strips_of(array):
    return jnp.concatenate(
        [array[:, part * strip : (part + 1) * strip] for part in range(array.shape[1] // strip)], axis=0
    )


def combine(own_ref, other_ref, order_ref, out_ref):
    summed = strips_of(own_ref[...] + other_ref[...].astype(f32)).astype(bf16)
    ordered = jnp.dot(order_ref[...], summed, preferred_element_type=f32).astype(bf16)
    out_ref[...] = ordered.reshape(out_ref.shape)


def norm_rows(arrived_ref, residual_ref, gain_ref, attn_ref, hidden_ref, out_ref, natural, stripped):
    rows, width = residual_ref.shape
    strips = width // strip
    summed = jnp.sum(arrived_ref[...].astype(f32), axis=0)
    for row in range(rows):
        for part in range(strips):
            at = row * strips + part
            natural[row : row + 1, part * strip : (part + 1) * strip] = summed[at : at + 1]
    projected = natural[0:rows, :]
    attn_ref[...] = projected.astype(bf16)
    hidden = residual_ref[...].astype(f32) + projected
    hidden_ref[...] = hidden
    scale = lax.rsqrt(jnp.mean(hidden * hidden, axis=1, keepdims=True) + norm_eps)
    normed = hidden * scale * gain_ref[...].reshape(1, width)
    stripped[...] = jnp.zeros_like(stripped)
    for row in range(rows):
        for part in range(strips):
            at = row * strips + part
            stripped[at : at + 1, :] = normed[row : row + 1, part * strip : (part + 1) * strip]
    tile = stripped[...].astype(bf16)
    for chip in range(out_ref.shape[0]):
        out_ref[chip] = tile


def run_expert(rows, own_rows_ref, other_rows_ref, back_ref, ids_ref, route_ref, gate_ref, up_ref, down_ref, own_ref, other_ref):
    chips, height, _ = own_rows_ref.shape
    half_rows = chips * rows
    strips = gate_ref.shape[0] // strip
    me = lax.axis_index("ctx")
    ordered = [
        jnp.dot(back_ref[...], ref[...].reshape(chips * height, strip), preferred_element_type=f32)
        for ref in (own_rows_ref, other_rows_ref)
    ]
    inputs = jnp.concatenate(
        [
            jnp.concatenate([part[at * half_rows : (at + 1) * half_rows] for part in ordered], axis=0)
            for at in range(strips)
        ],
        axis=1,
    ).astype(bf16)
    row = lax.broadcasted_iota(jnp.int32, (1, 2 * half_rows), 1)
    device = sum((row >= step * rows).astype(jnp.int32) for step in range(1, 2 * chips))
    other = (lax.rem(device, 2) != lax.rem(me, 2)).astype(jnp.int32)
    target = other * half_rows + lax.shift_right_logical(device, 1) * rows + row - device * rows
    named = jnp.sum(jnp.where(ids_ref[...] == me, route_ref[...], 0.0), axis=0, keepdims=True)
    place = lax.broadcasted_iota(jnp.int32, (2 * half_rows, 2 * half_rows), 0)
    weight = jnp.sum(jnp.where(place == target, named, 0.0), axis=1, keepdims=True)
    gate = jnp.dot(inputs, gate_ref[...], preferred_element_type=f32)
    up = jnp.dot(inputs, up_ref[...], preferred_element_type=f32)
    hidden = (gate * (1.0 / (1.0 + jnp.exp(-gate))) * up).astype(bf16)
    result = jnp.dot(hidden, down_ref[...], preferred_element_type=f32)
    result = jnp.where(weight > 0.0, result * weight, 0.0)
    own_ref[...] = result[:half_rows]
    other_ref[...] = result[half_rows:].astype(bf16)


def add_mixture(arrived_ref, hidden_ref, out_ref, natural):
    rows, width = hidden_ref.shape
    strips = width // strip
    mixture = jnp.sum(arrived_ref[...].astype(f32), axis=0)
    for row in range(rows):
        for part in range(strips):
            at = row * strips + part
            natural[row : row + 1, part * strip : (part + 1) * strip] = mixture[at : at + 1]
    out_ref[...] = (hidden_ref[...] + natural[0:rows, :]).astype(bf16)


def kernel_layer(
    query_latent,
    query_rope,
    cache_latent,
    cache_rope,
    valid_len,
    w_vo,
    residual,
    norm_gain,
    expert_ids,
    route_weight,
    w_gate,
    w_up,
    w_down,
):
    devices = lax.axis_size("ctx")
    rows, width = residual.shape
    block_len, latent = cache_latent.shape
    rope_dim = cache_rope.shape[0]
    head_count = query_rope.shape[1] // rope_dim
    total_rows = rows * devices
    heads_each = head_count // share
    groups = devices // share
    per = rows * heads_each
    strips = width // strip
    height = 8 * -(-rows * strips // 8)

    def swap(array, mask):
        return lax.ppermute(array, "ctx", [(d, d ^ mask) for d in range(devices)])

    tiles = 2 * per // 8 * 2 + 1
    flat = heads_each * total_rows
    outgoing = call(
        functools.partial(prepare, heads_each),
        jax.ShapeDtypeStruct((devices, tiles, 8, 128), bf16),
        query_latent,
        query_rope,
        scratch=[VMEM((share, 2 * per, latent // 2), f32), VMEM((share, 16, 128), f32)],
    )
    near = swap(cache_latent, 2)
    rope, outgoing = lax.optimization_barrier((cache_rope, outgoing))
    near_rope = swap(rope, 2)
    core, core_rope = swap(cache_latent, 1), swap(rope, 1)
    arrived = lax.all_to_all(outgoing, "ctx", split_axis=0, concat_axis=0, tiled=True)
    near, near_rope, arrived = lax.optimization_barrier((near, near_rope, arrived))
    far, far_rope = swap(near, 1), swap(near_rope, 1)
    query, rope_query, scores, limits = call(
        functools.partial(score_near, rows, heads_each),
        (
            jax.ShapeDtypeStruct((flat, latent), bf16),
            jax.ShapeDtypeStruct((flat, 256), bf16),
            jax.ShapeDtypeStruct((2, flat, block_len), f32),
            jax.ShapeDtypeStruct((total_rows, 128), jnp.int32),
        ),
        arrived,
        valid_len,
        cache_latent,
        cache_rope,
        core,
        core_rope,
        spaces={1: SMEM},
    )
    partial = call(
        functools.partial(attend, heads_each),
        jax.ShapeDtypeStruct((heads_each, total_rows + 8, latent), bf16),
        query,
        rope_query,
        scores,
        limits,
        cache_latent,
        core,
        near,
        far,
        near_rope,
        far_rope,
        scratch=[VMEM((2, flat, block_len), f32)],
    )
    lines = [[share * g + p for g in range(groups)] for p in range(share)]
    chips = devices // 2
    half_rows = rows * chips
    same_core = [[2 * chip + c for chip in range(chips)] for c in range(2)]
    send = strip_order(rows, chips, strips, height)
    send_order, back_order = jnp.asarray(send, bf16), jnp.asarray(send.T, bf16)
    strip_shape = jax.ShapeDtypeStruct((chips, height, strip), bf16)
    halves = (
        jax.ShapeDtypeStruct((half_rows, width), f32),
        jax.ShapeDtypeStruct((half_rows, width), bf16),
    )

    def exchange(array, partners):
        return lax.all_to_all(array, "ctx", split_axis=0, concat_axis=0, axis_index_groups=partners, tiled=True)

    pieces = exchange(partial, lines)
    kept, given = call(
        merge_project,
        halves,
        pieces,
        w_vo,
        scratch=[VMEM((total_rows, latent), f32), VMEM((2, half_rows, width), f32)],
    )
    columns = call(combine, strip_shape, kept, swap(given, 1), send_order)
    attn_out, hidden_state, normed = call(
        norm_rows,
        (
            jax.ShapeDtypeStruct((rows, width), bf16),
            jax.ShapeDtypeStruct((rows, width), f32),
            strip_shape,
        ),
        exchange(columns, same_core),
        residual,
        norm_gain,
        scratch=[VMEM((8, width), f32), VMEM((height, strip), f32)],
    )
    inputs = exchange(normed, same_core)
    kept, given = call(
        functools.partial(run_expert, rows),
        halves,
        inputs,
        swap(inputs, 1),
        back_order,
        expert_ids.T,
        route_weight.T,
        w_gate[0],
        w_up[0],
        w_down[0],
    )
    results = call(combine, strip_shape, kept, swap(given, 1), send_order)
    layer_out = call(
        add_mixture,
        jax.ShapeDtypeStruct((rows, width), bf16),
        exchange(results, same_core),
        hidden_state,
        scratch=[VMEM((8, width), f32)],
    )
    return attn_out, layer_out


def fits(mesh, query_rope, residual, cache_latent, cache_rope):
    devices = mesh.shape["ctx"]
    rope_dim = cache_rope.shape[0] // mesh.shape["groups"]
    heads = query_rope.shape[1] // rope_dim
    rows = residual.shape[0] // (devices * mesh.shape["groups"])
    per = rows * heads // share
    return (
        heads == devices
        and devices % share == 0
        and rope_dim == 64
        and 2 * per % 8 == 0
        and 8 <= per <= 16
        and rows * devices % 16 == 0
        and rows * devices <= 128
        and cache_latent.shape[1] == 512
        and cache_latent.shape[0] // (devices * mesh.shape["groups"]) == 512
        and devices & (devices - 1) == 0
        and residual.shape[1] % strip == 0
    )


def solution(mesh):
    in_specs = (
        P(("groups", "ctx"), None),
        P(("groups", "ctx"), None),
        P(("groups", "ctx"), None),
        P("groups", "ctx"),
        P("groups"),
        P("ctx", None),
        P(("groups", "ctx"), None),
        P(),
        P("groups", None),
        P("groups", None),
        P("ctx", None, None),
        P("ctx", None, None),
        P("ctx", None, None),
    )
    out_specs = (P(("groups", "ctx"), None), P(("groups", "ctx"), None))

    def layer(*args):
        body = kernel_layer if fits(mesh, args[1], args[6], args[2], args[3]) else plain_layer
        return jax.shard_map(body, mesh=mesh, in_specs=in_specs, out_specs=out_specs, check_vma=False)(*args)

    return layer
```

```python
import functools

import jax
import jax.numpy as jnp
import numpy as np
from jax import lax
from jax.experimental import pallas as pl
from jax.experimental.pallas import tpu as pltpu
from jax.sharding import PartitionSpec as P


softmax_scale = 192.0 ** (-0.5)
negative_fill = -1e30
norm_eps = 1e-06
share = 4
strip = 512

VMEM = pltpu.VMEM
SMEM = pltpu.SMEM
f32 = jnp.float32
bf16 = jnp.bfloat16


def expert_apply(inputs, gate_weight, up_weight, down_weight):
    gate_out = jnp.dot(inputs, gate_weight, preferred_element_type=jnp.float32)
    up_out = jnp.dot(inputs, up_weight, preferred_element_type=jnp.float32)
    hidden = (jax.nn.silu(gate_out) * up_out).astype(jnp.bfloat16)
    return jnp.dot(hidden, down_weight, preferred_element_type=jnp.float32).astype(jnp.bfloat16)


def plain_layer(
    query_latent,
    query_rope,
    cache_latent,
    cache_rope,
    valid_len,
    w_vo,
    residual,
    norm_gain,
    expert_ids,
    route_weight,
    w_gate,
    w_up,
    w_down,
):
    query_all, rope_all = (
        lax.all_gather(query_latent, "ctx", axis=0, tiled=True),
        lax.all_gather(query_rope, "ctx", axis=0, tiled=True),
    )
    total_rows = query_all.shape[0]
    own_rows = residual.shape[0]
    latent = cache_latent.shape[1]
    rope_dim = cache_rope.shape[0]
    head_count = rope_all.shape[1] // rope_dim
    block_len = cache_latent.shape[0]
    devices = lax.axis_size("ctx")
    self_index = lax.axis_index("ctx")
    col_count = head_count * latent // devices
    flat_query = query_all.reshape(total_rows * head_count, latent)
    flat_rope = rope_all.reshape(total_rows * head_count, rope_dim)
    scores = lax.dot_general(
        flat_query, cache_latent, (((1,), (1,)), ((), ())), preferred_element_type=jnp.float32
    )
    scores = (
        scores + jnp.dot(flat_rope, cache_rope, preferred_element_type=jnp.float32)
    ) * softmax_scale
    position = self_index * block_len + lax.broadcasted_iota(jnp.int32, (1, block_len), 1)
    usable = position < jnp.repeat(valid_len, head_count)[:, None]
    block_max = jnp.max(jnp.where(usable, scores, negative_fill), axis=1)
    weights = jnp.where(usable, jnp.exp(scores - block_max[:, None]), 0.0).astype(jnp.bfloat16)
    block_sum = jnp.sum(weights.astype(jnp.float32), axis=1)
    block_out = jnp.dot(weights, cache_latent, preferred_element_type=jnp.float32)
    row_max = block_max.reshape(total_rows, head_count)
    row_sum = block_sum.reshape(total_rows, head_count)
    global_max = lax.pmax(row_max, "ctx")
    factor = jnp.exp(row_max - global_max)
    scaled = (block_out.reshape(total_rows, head_count, latent) * factor[:, :, None]).reshape(
        total_rows, head_count * latent
    )
    merged = lax.psum_scatter(scaled, "ctx", scatter_dimension=1, tiled=True)
    totals = lax.psum(row_sum * factor, "ctx")
    divisor = lax.dynamic_slice_in_dim(totals, self_index * col_count // latent, 1, 1)
    attention = (merged / divisor).astype(jnp.bfloat16)
    projected = lax.psum_scatter(
        jnp.dot(attention, w_vo, preferred_element_type=jnp.float32),
        "ctx",
        scatter_dimension=0,
        tiled=True,
    )
    hidden_state = residual.astype(jnp.float32) + projected
    normed = (
        hidden_state
        * lax.rsqrt(jnp.mean(hidden_state * hidden_state, axis=1, keepdims=True) + norm_eps)
        * norm_gain
    ).astype(jnp.bfloat16)
    expert_iota = lax.broadcasted_iota(jnp.int32, (1, 1, devices), 2)
    route_table = jnp.sum(
        jnp.where(expert_ids[:, :, None] == expert_iota, route_weight[:, :, None], 0.0), axis=1
    )
    gate_own = w_gate[0]
    up_own = w_up[0]
    down_own = w_down[0]
    own_table = jnp.transpose(
        lax.dynamic_slice_in_dim(route_table, self_index * own_rows, own_rows, 0)
    )
    outgoing = jnp.where(
        own_table[:, :, None] > 0.0, normed[None, :, :], jnp.zeros((), jnp.bfloat16)
    )
    arrived = lax.all_to_all(outgoing, "ctx", split_axis=0, concat_axis=0, tiled=True)
    item_count = arrived.shape[1]
    stacked = arrived.reshape(devices * item_count, arrived.shape[2])
    result = expert_apply(stacked, gate_own, up_own, down_own).reshape(
        devices, item_count, arrived.shape[2]
    )
    returned = lax.all_to_all(result, "ctx", split_axis=0, concat_axis=0, tiled=True)
    mixture = jnp.sum(own_table[:, :, None] * returned.astype(jnp.float32), axis=0)
    layer_out = (hidden_state + mixture).astype(jnp.bfloat16)
    return (projected.astype(jnp.bfloat16), layer_out)


def place(device):
    return 2 * ((device // 2 ^ device // 4) & 1) + device % 2


def call(kernel, out_shape, *operands, spaces=None, scratch=(), limit=24):
    spaces = spaces or {}
    in_specs = [pl.BlockSpec(memory_space=spaces.get(i, VMEM)) for i in range(len(operands))]
    many = isinstance(out_shape, (tuple, list))
    out_specs = [pl.BlockSpec(memory_space=VMEM) for _ in out_shape] if many else pl.BlockSpec(memory_space=VMEM)
    return pl.pallas_call(
        kernel,
        out_shape=out_shape,
        in_specs=in_specs,
        out_specs=out_specs,
        scratch_shapes=list(scratch),
        compiler_params=pltpu.CompilerParams(vmem_limit_bytes=limit << 20),
        cost_estimate=pl.CostEstimate(flops=4 * 10**9, bytes_accessed=64 << 20, transcendentals=0),
    )(*operands)


def strip_order(rows, devices, strips, height):
    order = np.zeros((devices * height, strips * rows * devices), np.float32)
    for device in range(devices):
        for row in range(rows):
            for part in range(strips):
                order[device * height + row * strips + part, part * rows * devices + device * rows + row] = 1.0
    return order


def prepare(heads_each, query_hbm, rope_hbm, out_ref, query_ref, rope_ref, piece, rope_piece, arrive):
    copies = [
        pltpu.make_async_copy(query_hbm, query_ref, arrive.at[0]),
        pltpu.make_async_copy(rope_hbm, rope_ref, arrive.at[1]),
    ]
    for copy in copies:
        copy.start()
    rows = query_ref.shape[0]
    per = rows * heads_each
    latent = query_ref.shape[1] // (heads_each * share)
    rope_dim = rope_ref.shape[1] // (heads_each * share)
    half_width = latent // 2
    devices = out_ref.shape[0]
    lane = lax.broadcasted_iota(jnp.int32, (8, 128), 1)
    rope_piece[...] = jnp.zeros_like(rope_piece)
    for copy in copies:
        copy.wait()
    query = query_ref[...].astype(f32)
    rope = rope_ref[...].astype(f32)
    for kind in range(share):
        owners = [device for device in range(devices) if place(device) == kind]
        for item in range(per):
            row, index = divmod(item, heads_each)
            head = owners[index]
            for half in range(2):
                begin = head * latent + half * half_width
                piece[kind, half * per + item : half * per + item + 1, :] = query[row : row + 1, begin : begin + half_width]
            block = head * rope_dim // 128
            rope_piece[kind, item : item + 1, :] = rope[row : row + 1, block * 128 : (block + 1) * 128]
    for kind in range(share):
        first = rope_piece[kind, 0:8, :]
        second = rope_piece[kind, 8:16, :]
        if kind % 2 == 1:
            first = pltpu.roll(first, 64, 1)
        else:
            second = pltpu.roll(second, 64, 1)
        tail = jnp.where(lane < 64, first, second).astype(bf16)
        tiles = []
        for rt in range(2 * per // 8):
            for lt in range(half_width // 128):
                tiles.append(piece[kind, rt * 8 : (rt + 1) * 8, lt * 128 : (lt + 1) * 128].astype(bf16))
        tiles.append(tail)
        for device in range(devices):
            if place(device) == kind:
                for index, tile in enumerate(tiles):
                    out_ref[device, index] = tile


def place_of(item, source, rows, heads_each, total_rows):
    row = sum((item >= step * heads_each).astype(jnp.int32) for step in range(1, rows))
    head = item - row * heads_each
    core, chip = lax.rem(source, 2), lax.shift_right_logical(source, 1)
    return head * total_rows + core * (total_rows // 2) + chip * rows + row


def one_hot(target, height):
    return (lax.broadcasted_iota(jnp.int32, (height, target.shape[1]), 0) == target).astype(f32).astype(bf16)


def score_block(query, rope_query, keys, rope_keys, begin, limits, heads_each):
    flat, latent = query.shape
    total_rows = flat // heads_each
    block_len = rope_keys.shape[1]
    empty = jnp.zeros_like(rope_keys)
    rope_keys = jnp.concatenate([rope_keys, empty, empty, rope_keys], axis=0)
    scores = lax.dot_general(query, keys, (((1,), (1,)), ((), ())), preferred_element_type=f32)
    scores = (scores + jnp.dot(rope_query, rope_keys, preferred_element_type=f32)) * softmax_scale
    valid = lax.broadcasted_iota(jnp.int32, (total_rows, block_len), 1) + begin < limits
    return jnp.where(valid[None], scores.reshape(heads_each, total_rows, block_len), negative_fill).reshape(flat, block_len)


def score_near(rows, heads_each, arrived_ref, length_ref, own_ref, own_rope_ref, core_ref, core_rope_ref, query_ref, rope_query_ref, scores_ref, limit_ref):
    devices = arrived_ref.shape[0]
    total_rows = rows * devices
    flat = heads_each * total_rows
    per = rows * heads_each
    row_tiles = 2 * per // 8
    block_len, latent = own_ref.shape
    me = lax.axis_index("ctx")
    for row in range(total_rows):
        device, index = divmod(row, rows)
        at = device % 2 * (total_rows // 2) + device // 2 * rows + index
        limit_ref[at : at + 1, :] = jnp.full((1, 128), length_ref[row], jnp.int32)
    column = lax.broadcasted_iota(jnp.int32, (1, row_tiles * devices * 8), 1)
    source = lax.rem(lax.shift_right_logical(column, 3), devices)
    unit = lax.div(column, devices * 8) * 8 + lax.rem(column, 8)
    second = (unit >= per).astype(jnp.int32)
    target = second * flat + place_of(unit - second * per, source, rows, heads_each, total_rows)
    gathered = jnp.concatenate(
        [
            jnp.concatenate(
                [arrived_ref[:, 2 * rt + lt].reshape(devices * 8, 128) for lt in range(2)], axis=1
            )
            for rt in range(row_tiles)
        ],
        axis=0,
    )
    ordered = jnp.dot(one_hot(target, 2 * flat), gathered, preferred_element_type=f32).astype(bf16)
    query = jnp.concatenate([ordered[:flat], ordered[flat:]], axis=1)
    column = lax.broadcasted_iota(jnp.int32, (1, devices * 8), 1)
    source = lax.shift_right_logical(column, 3)
    item = lax.rem(column, 8)
    rope_rows = arrived_ref[:, 2 * row_tiles].reshape(devices * 8, 128)
    halves = []
    for half in range(2):
        shifted = item + 8 * half
        target = jnp.where(shifted < per, place_of(shifted, source, rows, heads_each, total_rows), -1)
        halves.append(jnp.dot(one_hot(target, flat), rope_rows, preferred_element_type=f32).astype(bf16))
    rope_query = jnp.concatenate(halves, axis=1)
    query_ref[...] = query
    rope_query_ref[...] = rope_query
    limits = limit_ref[...][:, 0:1]
    blocks = ((own_ref[...], own_rope_ref[...]), (core_ref[...], core_rope_ref[...]))
    for index, (keys, rope_keys) in enumerate(blocks):
        begin = lax.bitwise_xor(me, index) * block_len
        scores_ref[index] = score_block(query, rope_query, keys, rope_keys, begin, limits, heads_each)


def attend(heads_each, query_ref, rope_query_ref, scores_ref, limit_ref, own_ref, core_ref, near_ref, far_ref, near_rope_ref, far_rope_ref, out_ref, more_ref):
    flat, latent = query_ref.shape
    total_rows = flat // heads_each
    block_len = own_ref.shape[0]
    me = lax.axis_index("ctx")
    limits = limit_ref[...][:, 0:1]
    query, rope_query = query_ref[...], rope_query_ref[...]
    core = lax.rem(me, 2)
    owners = [me, lax.bitwise_xor(me, 1), lax.bitwise_xor(me, 2 + 2 * core), lax.bitwise_xor(me, 5 - 2 * core)]
    highest = jnp.maximum(
        jnp.max(scores_ref[0], axis=1, keepdims=True), jnp.max(scores_ref[1], axis=1, keepdims=True)
    )
    for index, (block, rope_block) in enumerate(((near_ref, near_rope_ref), (far_ref, far_rope_ref))):
        begin = owners[index + 2] * block_len
        scores = score_block(query, rope_query, block[...], rope_block[...], begin, limits, heads_each)
        more_ref[index] = scores
        highest = jnp.maximum(highest, jnp.max(scores, axis=1, keepdims=True))
    total = None
    summed = None
    for index, block in enumerate((own_ref, core_ref, near_ref, far_ref)):
        begin = owners[index] * block_len
        valid = lax.broadcasted_iota(jnp.int32, (total_rows, block_len), 1) + begin < limits
        scores = scores_ref[index] if index < 2 else more_ref[index - 2]
        weights = jnp.exp(scores - highest)
        weights = jnp.where(valid[None], weights.reshape(heads_each, total_rows, block_len), 0.0).reshape(flat, block_len)
        weights = weights.astype(bf16)
        part = jnp.sum(weights.astype(f32), axis=1, keepdims=True)
        summed = part if summed is None else summed + part
        part = jnp.dot(weights, block[...], preferred_element_type=f32)
        total = part if total is None else total + part
    lane = lax.broadcasted_iota(jnp.int32, (8, 128), 1)
    for head in range(heads_each):
        base = head * total_rows
        out_ref[head, 0:total_rows, :] = total[base : base + total_rows].astype(bf16)
        note = jnp.zeros((8, 128), f32)
        for tile in range(total_rows // 8):
            for offset, value in ((0, highest), (3, summed)):
                value = jnp.broadcast_to(value[base + tile * 8 : base + tile * 8 + 8], (8, 128))
                for piece in range(3):
                    rounded = value.astype(bf16).astype(f32)
                    note = jnp.where(lane == 8 * tile + offset + piece, rounded, note)
                    value = value - rounded
        wide = jnp.concatenate([note, jnp.zeros((8, out_ref.shape[2] - 128), f32)], axis=1)
        out_ref[head, total_rows:, :] = wide.astype(bf16)


def merge_project(arrived_ref, weight_ref, own_ref, other_ref, attention_ref, product_ref):
    sources, height, latent = arrived_ref.shape
    total_rows = height - 8
    peaks = []
    sums = []
    for source in range(sources):
        note = arrived_ref[source, total_rows:, 0:128].astype(f32)
        shifted = [note] + [pltpu.roll(note, 128 - step, 1) for step in range(1, 6)]
        peaks.append(shifted[0] + shifted[1] + shifted[2])
        sums.append(shifted[3] + shifted[4] + shifted[5])
    highest = functools.reduce(jnp.maximum, peaks)
    factors = [jnp.exp(peak - highest) for peak in peaks]
    divisor = sum(factor * part for factor, part in zip(factors, sums))
    factors = [factor / divisor for factor in factors]
    for tile in range(total_rows // 8):
        span = slice(tile * 8, tile * 8 + 8)
        attention_ref[span, :] = sum(
            factor[:, 8 * tile : 8 * tile + 1] * arrived_ref[source, span, :].astype(f32)
            for source, factor in enumerate(factors)
        )
    product = jnp.dot(attention_ref[...].astype(bf16), weight_ref[...], preferred_element_type=f32)
    product_ref[...] = product.reshape(product_ref.shape)
    core = lax.rem(lax.axis_index("ctx"), 2)
    own_ref[...] = product_ref[core]
    other_ref[...] = product_ref[1 - core].astype(bf16)


def strips_of(array):
    return jnp.concatenate(
        [array[:, part * strip : (part + 1) * strip] for part in range(array.shape[1] // strip)], axis=0
    )


def combine(own_ref, other_ref, order_ref, out_ref):
    summed = strips_of(own_ref[...] + other_ref[...].astype(f32)).astype(bf16)
    ordered = jnp.dot(order_ref[...], summed, preferred_element_type=f32).astype(bf16)
    out_ref[...] = ordered.reshape(out_ref.shape)


def norm_rows(arrived_ref, residual_ref, gain_ref, attn_ref, hidden_ref, out_ref, natural, stripped):
    rows, width = residual_ref.shape
    strips = width // strip
    summed = jnp.sum(arrived_ref[...].astype(f32), axis=0)
    for row in range(rows):
        for part in range(strips):
            at = row * strips + part
            natural[row : row + 1, part * strip : (part + 1) * strip] = summed[at : at + 1]
    projected = natural[0:rows, :]
    attn_ref[...] = projected.astype(bf16)
    hidden = residual_ref[...].astype(f32) + projected
    hidden_ref[...] = hidden
    scale = lax.rsqrt(jnp.mean(hidden * hidden, axis=1, keepdims=True) + norm_eps)
    normed = hidden * scale * gain_ref[...].reshape(1, width)
    stripped[...] = jnp.zeros_like(stripped)
    for row in range(rows):
        for part in range(strips):
            at = row * strips + part
            stripped[at : at + 1, :] = normed[row : row + 1, part * strip : (part + 1) * strip]
    tile = stripped[...].astype(bf16)
    for chip in range(out_ref.shape[0]):
        out_ref[chip] = tile


def run_expert(rows, own_rows_ref, other_rows_ref, back_ref, ids_ref, route_ref, gate_ref, up_ref, down_ref, own_ref, other_ref):
    chips, height, _ = own_rows_ref.shape
    half_rows = chips * rows
    strips = gate_ref.shape[0] // strip
    me = lax.axis_index("ctx")
    ordered = [
        jnp.dot(back_ref[...], ref[...].reshape(chips * height, strip), preferred_element_type=f32)
        for ref in (own_rows_ref, other_rows_ref)
    ]
    inputs = jnp.concatenate(
        [
            jnp.concatenate([part[at * half_rows : (at + 1) * half_rows] for part in ordered], axis=0)
            for at in range(strips)
        ],
        axis=1,
    ).astype(bf16)
    row = lax.broadcasted_iota(jnp.int32, (1, 2 * half_rows), 1)
    device = sum((row >= step * rows).astype(jnp.int32) for step in range(1, 2 * chips))
    other = (lax.rem(device, 2) != lax.rem(me, 2)).astype(jnp.int32)
    target = other * half_rows + lax.shift_right_logical(device, 1) * rows + row - device * rows
    named = jnp.sum(jnp.where(ids_ref[...] == me, route_ref[...], 0.0), axis=0, keepdims=True)
    place = lax.broadcasted_iota(jnp.int32, (2 * half_rows, 2 * half_rows), 0)
    weight = jnp.sum(jnp.where(place == target, named, 0.0), axis=1, keepdims=True)
    gate = jnp.dot(inputs, gate_ref[...], preferred_element_type=f32)
    up = jnp.dot(inputs, up_ref[...], preferred_element_type=f32)
    hidden = (gate * (1.0 / (1.0 + jnp.exp(-gate))) * up).astype(bf16)
    result = jnp.dot(hidden, down_ref[...], preferred_element_type=f32)
    result = jnp.where(weight > 0.0, result * weight, 0.0)
    own_ref[...] = result[:half_rows]
    other_ref[...] = result[half_rows:].astype(bf16)


def add_mixture(arrived_ref, hidden_ref, out_ref, natural):
    rows, width = hidden_ref.shape
    strips = width // strip
    mixture = jnp.sum(arrived_ref[...].astype(f32), axis=0)
    for row in range(rows):
        for part in range(strips):
            at = row * strips + part
            natural[row : row + 1, part * strip : (part + 1) * strip] = mixture[at : at + 1]
    out_ref[...] = (hidden_ref[...] + natural[0:rows, :]).astype(bf16)


def kernel_layer(
    query_latent,
    query_rope,
    cache_latent,
    cache_rope,
    valid_len,
    w_vo,
    residual,
    norm_gain,
    expert_ids,
    route_weight,
    w_gate,
    w_up,
    w_down,
):
    devices = lax.axis_size("ctx")
    rows, width = residual.shape
    block_len, latent = cache_latent.shape
    rope_dim = cache_rope.shape[0]
    head_count = query_rope.shape[1] // rope_dim
    total_rows = rows * devices
    heads_each = head_count // share
    per = rows * heads_each
    strips = width // strip
    height = 8 * -(-rows * strips // 8)

    def swap(array):
        return lax.ppermute(array, "ctx", [(d, d ^ 1) for d in range(devices)])

    def trade(array):
        return lax.ppermute(array, "ctx", [(d, d ^ (2 + d % 2 * 2)) for d in range(devices)])

    tiles = 2 * per // 8 * 2 + 1
    flat = heads_each * total_rows
    outgoing = call(
        functools.partial(prepare, heads_each),
        jax.ShapeDtypeStruct((devices, tiles, 8, 128), bf16),
        query_latent,
        query_rope,
        spaces={0: pltpu.HBM, 1: pltpu.HBM},
        limit=60,
        scratch=[
            VMEM(query_latent.shape, bf16),
            VMEM(query_rope.shape, bf16),
            VMEM((share, 2 * per, latent // 2), f32),
            VMEM((share, 16, 128), f32),
            pltpu.SemaphoreType.DMA((2,)),
        ],
    )
    near = trade(cache_latent)
    rope, outgoing = lax.optimization_barrier((cache_rope, outgoing))
    core, core_rope, near_rope = swap(cache_latent), swap(rope), trade(rope)
    arrived = lax.all_to_all(outgoing, "ctx", split_axis=0, concat_axis=0, tiled=True)
    near, near_rope, core, core_rope, arrived = lax.optimization_barrier((near, near_rope, core, core_rope, arrived))
    far, far_rope = swap(near), swap(near_rope)
    query, rope_query, scores, limits = call(
        functools.partial(score_near, rows, heads_each),
        (
            jax.ShapeDtypeStruct((flat, latent), bf16),
            jax.ShapeDtypeStruct((flat, 256), bf16),
            jax.ShapeDtypeStruct((2, flat, block_len), f32),
            jax.ShapeDtypeStruct((total_rows, 128), jnp.int32),
        ),
        arrived,
        valid_len,
        cache_latent,
        cache_rope,
        core,
        core_rope,
        spaces={1: SMEM},
    )
    partial = call(
        functools.partial(attend, heads_each),
        jax.ShapeDtypeStruct((heads_each, total_rows + 8, latent), bf16),
        query,
        rope_query,
        scores,
        limits,
        cache_latent,
        core,
        near,
        far,
        near_rope,
        far_rope,
        scratch=[VMEM((2, flat, block_len), f32)],
    )
    lines = [[d for d in range(devices) if place(d) == kind] for kind in range(share)]
    chips = devices // 2
    half_rows = rows * chips
    same_core = [[2 * chip + c for chip in range(chips)] for c in range(2)]
    send = strip_order(rows, chips, strips, height)
    send_order, back_order = jnp.asarray(send, bf16), jnp.asarray(send.T, bf16)
    strip_shape = jax.ShapeDtypeStruct((chips, height, strip), bf16)
    halves = (
        jax.ShapeDtypeStruct((half_rows, width), f32),
        jax.ShapeDtypeStruct((half_rows, width), bf16),
    )

    def exchange(array, partners):
        return lax.all_to_all(array, "ctx", split_axis=0, concat_axis=0, axis_index_groups=partners, tiled=True)

    pieces = exchange(partial, lines)
    kept, given = call(
        merge_project,
        halves,
        pieces,
        w_vo,
        scratch=[VMEM((total_rows, latent), f32), VMEM((2, half_rows, width), f32)],
    )
    columns = call(combine, strip_shape, kept, swap(given), send_order)
    attn_out, hidden_state, normed = call(
        norm_rows,
        (
            jax.ShapeDtypeStruct((rows, width), bf16),
            jax.ShapeDtypeStruct((rows, width), f32),
            strip_shape,
        ),
        exchange(columns, same_core),
        residual,
        norm_gain,
        scratch=[VMEM((8, width), f32), VMEM((height, strip), f32)],
    )
    inputs = exchange(normed, same_core)
    kept, given = call(
        functools.partial(run_expert, rows),
        halves,
        inputs,
        swap(inputs),
        back_order,
        expert_ids.T,
        route_weight.T,
        w_gate[0],
        w_up[0],
        w_down[0],
    )
    results = call(combine, strip_shape, kept, swap(given), send_order)
    layer_out = call(
        add_mixture,
        jax.ShapeDtypeStruct((rows, width), bf16),
        exchange(results, same_core),
        hidden_state,
        scratch=[VMEM((8, width), f32)],
    )
    return attn_out, layer_out


def fits(mesh, query_rope, residual, cache_latent, cache_rope):
    devices = mesh.shape["ctx"]
    rope_dim = cache_rope.shape[0] // mesh.shape["groups"]
    heads = query_rope.shape[1] // rope_dim
    rows = residual.shape[0] // (devices * mesh.shape["groups"])
    per = rows * heads // share
    return (
        heads == devices
        and devices % (2 * share) == 0
        and rope_dim == 64
        and 2 * per % 8 == 0
        and 8 <= per <= 16
        and rows * devices % 16 == 0
        and rows * devices <= 128
        and cache_latent.shape[1] == 512
        and cache_latent.shape[0] // (devices * mesh.shape["groups"]) == 512
        and devices & (devices - 1) == 0
        and residual.shape[1] % strip == 0
    )


def solution(mesh):
    in_specs = (
        P(("groups", "ctx"), None),
        P(("groups", "ctx"), None),
        P(("groups", "ctx"), None),
        P("groups", "ctx"),
        P("groups"),
        P("ctx", None),
        P(("groups", "ctx"), None),
        P(),
        P("groups", None),
        P("groups", None),
        P("ctx", None, None),
        P("ctx", None, None),
        P("ctx", None, None),
    )
    out_specs = (P(("groups", "ctx"), None), P(("groups", "ctx"), None))

    def layer(*args):
        body = kernel_layer if fits(mesh, args[1], args[6], args[2], args[3]) else plain_layer
        return jax.shard_map(body, mesh=mesh, in_specs=in_specs, out_specs=out_specs, check_vma=False)(*args)

    return layer
```

```python
import functools
import math

import jax
import jax.numpy as jnp
import numpy as np
from jax import lax
from jax.experimental import pallas as pl
from jax.experimental.pallas import tpu as pltpu
from jax.sharding import PartitionSpec as P


softmax_scale = 192.0 ** (-0.5)
negative_fill = -1e30
norm_eps = 1e-06
exponent_scale = softmax_scale * math.log2(math.e)
no_position = -1e29
share = 4
strip = 512

VMEM = pltpu.VMEM
SMEM = pltpu.SMEM
f32 = jnp.float32
bf16 = jnp.bfloat16


def expert_apply(inputs, gate_weight, up_weight, down_weight):
    gate_out = jnp.dot(inputs, gate_weight, preferred_element_type=jnp.float32)
    up_out = jnp.dot(inputs, up_weight, preferred_element_type=jnp.float32)
    hidden = (jax.nn.silu(gate_out) * up_out).astype(jnp.bfloat16)
    return jnp.dot(hidden, down_weight, preferred_element_type=jnp.float32).astype(jnp.bfloat16)


def plain_layer(
    query_latent,
    query_rope,
    cache_latent,
    cache_rope,
    valid_len,
    w_vo,
    residual,
    norm_gain,
    expert_ids,
    route_weight,
    w_gate,
    w_up,
    w_down,
):
    query_all, rope_all = (
        lax.all_gather(query_latent, "ctx", axis=0, tiled=True),
        lax.all_gather(query_rope, "ctx", axis=0, tiled=True),
    )
    total_rows = query_all.shape[0]
    own_rows = residual.shape[0]
    latent = cache_latent.shape[1]
    rope_dim = cache_rope.shape[0]
    head_count = rope_all.shape[1] // rope_dim
    block_len = cache_latent.shape[0]
    devices = lax.axis_size("ctx")
    self_index = lax.axis_index("ctx")
    col_count = head_count * latent // devices
    flat_query = query_all.reshape(total_rows * head_count, latent)
    flat_rope = rope_all.reshape(total_rows * head_count, rope_dim)
    scores = lax.dot_general(
        flat_query, cache_latent, (((1,), (1,)), ((), ())), preferred_element_type=jnp.float32
    )
    scores = (
        scores + jnp.dot(flat_rope, cache_rope, preferred_element_type=jnp.float32)
    ) * softmax_scale
    position = self_index * block_len + lax.broadcasted_iota(jnp.int32, (1, block_len), 1)
    usable = position < jnp.repeat(valid_len, head_count)[:, None]
    block_max = jnp.max(jnp.where(usable, scores, negative_fill), axis=1)
    weights = jnp.where(usable, jnp.exp(scores - block_max[:, None]), 0.0).astype(jnp.bfloat16)
    block_sum = jnp.sum(weights.astype(jnp.float32), axis=1)
    block_out = jnp.dot(weights, cache_latent, preferred_element_type=jnp.float32)
    row_max = block_max.reshape(total_rows, head_count)
    row_sum = block_sum.reshape(total_rows, head_count)
    global_max = lax.pmax(row_max, "ctx")
    factor = jnp.exp(row_max - global_max)
    scaled = (block_out.reshape(total_rows, head_count, latent) * factor[:, :, None]).reshape(
        total_rows, head_count * latent
    )
    merged = lax.psum_scatter(scaled, "ctx", scatter_dimension=1, tiled=True)
    totals = lax.psum(row_sum * factor, "ctx")
    divisor = lax.dynamic_slice_in_dim(totals, self_index * col_count // latent, 1, 1)
    attention = (merged / divisor).astype(jnp.bfloat16)
    projected = lax.psum_scatter(
        jnp.dot(attention, w_vo, preferred_element_type=jnp.float32),
        "ctx",
        scatter_dimension=0,
        tiled=True,
    )
    hidden_state = residual.astype(jnp.float32) + projected
    normed = (
        hidden_state
        * lax.rsqrt(jnp.mean(hidden_state * hidden_state, axis=1, keepdims=True) + norm_eps)
        * norm_gain
    ).astype(jnp.bfloat16)
    expert_iota = lax.broadcasted_iota(jnp.int32, (1, 1, devices), 2)
    route_table = jnp.sum(
        jnp.where(expert_ids[:, :, None] == expert_iota, route_weight[:, :, None], 0.0), axis=1
    )
    gate_own = w_gate[0]
    up_own = w_up[0]
    down_own = w_down[0]
    own_table = jnp.transpose(
        lax.dynamic_slice_in_dim(route_table, self_index * own_rows, own_rows, 0)
    )
    outgoing = jnp.where(
        own_table[:, :, None] > 0.0, normed[None, :, :], jnp.zeros((), jnp.bfloat16)
    )
    arrived = lax.all_to_all(outgoing, "ctx", split_axis=0, concat_axis=0, tiled=True)
    item_count = arrived.shape[1]
    stacked = arrived.reshape(devices * item_count, arrived.shape[2])
    result = expert_apply(stacked, gate_own, up_own, down_own).reshape(
        devices, item_count, arrived.shape[2]
    )
    returned = lax.all_to_all(result, "ctx", split_axis=0, concat_axis=0, tiled=True)
    mixture = jnp.sum(own_table[:, :, None] * returned.astype(jnp.float32), axis=0)
    layer_out = (hidden_state + mixture).astype(jnp.bfloat16)
    return (projected.astype(jnp.bfloat16), layer_out)


def place(device):
    return 2 * ((device // 2 ^ device // 4) & 1) + device % 2


def call(kernel, out_shape, *operands, spaces=None, scratch=(), limit=24, out_space=VMEM):
    spaces = spaces or {}
    in_specs = [pl.BlockSpec(memory_space=spaces.get(i, VMEM)) for i in range(len(operands))]
    many = isinstance(out_shape, (tuple, list))
    out_specs = [pl.BlockSpec(memory_space=VMEM) for _ in out_shape] if many else pl.BlockSpec(memory_space=out_space)
    return pl.pallas_call(
        kernel,
        out_shape=out_shape,
        in_specs=in_specs,
        out_specs=out_specs,
        scratch_shapes=list(scratch),
        compiler_params=pltpu.CompilerParams(vmem_limit_bytes=limit << 20),
        cost_estimate=pl.CostEstimate(flops=4 * 10**9, bytes_accessed=64 << 20, transcendentals=0),
    )(*operands)


def strip_order(rows, devices, strips, height):
    order = np.zeros((devices * height, strips * rows * devices), np.float32)
    for device in range(devices):
        for row in range(rows):
            for part in range(strips):
                order[device * height + row * strips + part, part * rows * devices + device * rows + row] = 1.0
    return order


def prepare(heads_each, query_hbm, rope_hbm, out_hbm, query_ref, rope_ref, piece, rope_piece, packed, arrive, leave):
    fetches = [
        pltpu.make_async_copy(query_hbm, query_ref, arrive.at[0]),
        pltpu.make_async_copy(rope_hbm, rope_ref, arrive.at[1]),
    ]
    for fetch in fetches:
        fetch.start()
    rows = query_ref.shape[0]
    per = rows * heads_each
    latent = query_ref.shape[1] // (heads_each * share)
    rope_dim = rope_ref.shape[1] // (heads_each * share)
    half_width = latent // 2
    devices = out_hbm.shape[0]
    lane = lax.broadcasted_iota(jnp.int32, (8, 128), 1)
    rope_piece[...] = jnp.zeros_like(rope_piece)
    for fetch in fetches:
        fetch.wait()
    query = query_ref[...].astype(f32)
    rope = rope_ref[...].astype(f32)
    sends = []
    for kind in range(share):
        owners = [device for device in range(devices) if place(device) == kind]
        for item in range(per):
            row, index = divmod(item, heads_each)
            head = owners[index]
            for half in range(2):
                begin = head * latent + half * half_width
                piece[kind, half * per + item : half * per + item + 1, :] = query[row : row + 1, begin : begin + half_width]
            block = head * rope_dim // 128
            rope_piece[kind, item : item + 1, :] = rope[row : row + 1, block * 128 : (block + 1) * 128]
        first = rope_piece[kind, 0:8, :]
        second = rope_piece[kind, 8:16, :]
        if kind % 2 == 1:
            first = pltpu.roll(first, 64, 1)
        else:
            second = pltpu.roll(second, 64, 1)
        row_tiles, lane_tiles = 2 * per // 8, half_width // 128
        for rt in range(row_tiles):
            for lt in range(lane_tiles):
                tile = piece[kind, rt * 8 : (rt + 1) * 8, lt * 128 : (lt + 1) * 128]
                packed[kind, rt * lane_tiles + lt] = tile.astype(bf16)
        packed[kind, row_tiles * lane_tiles] = jnp.where(lane < 64, first, second).astype(bf16)
        for device in owners:
            send = pltpu.make_async_copy(packed.at[kind], out_hbm.at[device], leave.at[device])
            send.start()
            sends.append(send)
    for send in sends:
        send.wait()


def place_of(item, source, rows, heads_each, total_rows):
    row = sum((item >= step * heads_each).astype(jnp.int32) for step in range(1, rows))
    head = item - row * heads_each
    core, chip = lax.rem(source, 2), lax.shift_right_logical(source, 1)
    return head * total_rows + core * (total_rows // 2) + chip * rows + row


def one_hot(target, height):
    return (lax.broadcasted_iota(jnp.int32, (height, target.shape[1]), 0) == target).astype(f32).astype(bf16)


def tables(rows, heads_each, length_ref, order_ref, rope_order_ref, limit_ref):
    total_rows = limit_ref.shape[0]
    devices = total_rows // rows
    flat = heads_each * total_rows
    per = rows * heads_each
    for row in range(total_rows):
        device, index = divmod(row, rows)
        at = device % 2 * (total_rows // 2) + device // 2 * rows + index
        limit_ref[at : at + 1, :] = jnp.full((1, 128), length_ref[row], jnp.int32)
    column = lax.broadcasted_iota(jnp.int32, (1, order_ref.shape[1]), 1)
    source = lax.rem(lax.shift_right_logical(column, 3), devices)
    unit = lax.div(column, devices * 8) * 8 + lax.rem(column, 8)
    second = (unit >= per).astype(jnp.int32)
    target = second * flat + place_of(unit - second * per, source, rows, heads_each, total_rows)
    order_ref[...] = one_hot(target, 2 * flat)
    column = lax.broadcasted_iota(jnp.int32, (1, devices * 8), 1)
    source = lax.shift_right_logical(column, 3)
    item = lax.rem(column, 8)
    for half in range(2):
        shifted = item + 8 * half
        target = jnp.where(shifted < per, place_of(shifted, source, rows, heads_each, total_rows), -1)
        rope_order_ref[half * flat : (half + 1) * flat, :] = one_hot(target, flat)


def score_block(query, rope_query, keys, rope_keys, begin, limits, heads_each):
    flat, _ = query.shape
    total_rows = flat // heads_each
    block_len = rope_keys.shape[1]
    empty = jnp.zeros_like(rope_keys)
    rope_keys = jnp.concatenate([rope_keys, empty, empty, rope_keys], axis=0)
    scores = lax.dot_general(query, keys, (((1,), (1,)), ((), ())), preferred_element_type=f32)
    scores = scores + jnp.dot(rope_query, rope_keys, preferred_element_type=f32)
    valid = lax.broadcasted_iota(jnp.int32, (total_rows, block_len), 1) + begin < limits
    return jnp.where(valid[None], scores.reshape(heads_each, total_rows, block_len), negative_fill).reshape(flat, block_len)


def score_near(heads_each, arrived_ref, order_ref, rope_order_ref, limit_ref, own_ref, own_rope_ref, core_ref, core_rope_ref, query_ref, rope_query_ref, scores_ref):
    devices = arrived_ref.shape[0]
    flat = order_ref.shape[0] // 2
    row_tiles = arrived_ref.shape[1] // 2
    block_len, _ = own_ref.shape
    me = lax.axis_index("ctx")
    gathered = jnp.concatenate(
        [
            jnp.concatenate(
                [arrived_ref[:, 2 * rt + lt].reshape(devices * 8, 128) for lt in range(2)], axis=1
            )
            for rt in range(row_tiles)
        ],
        axis=0,
    )
    ordered = jnp.dot(order_ref[...], gathered, preferred_element_type=f32).astype(bf16)
    query = jnp.concatenate([ordered[:flat], ordered[flat:]], axis=1)
    rope_rows = arrived_ref[:, 2 * row_tiles].reshape(devices * 8, 128)
    ordered = jnp.dot(rope_order_ref[...], rope_rows, preferred_element_type=f32).astype(bf16)
    rope_query = jnp.concatenate([ordered[:flat], ordered[flat:]], axis=1)
    query_ref[...] = query
    rope_query_ref[...] = rope_query
    limits = limit_ref[...][:, 0:1]
    blocks = ((own_ref[...], own_rope_ref[...]), (core_ref[...], core_rope_ref[...]))
    for index, (keys, rope_keys) in enumerate(blocks):
        begin = lax.bitwise_xor(me, index) * block_len
        scores_ref[index] = score_block(query, rope_query, keys, rope_keys, begin, limits, heads_each)


def attend(heads_each, query_ref, rope_query_ref, scores_ref, limit_ref, own_ref, core_ref, near_ref, far_ref, near_rope_ref, far_rope_ref, out_ref, more_ref):
    flat, _ = query_ref.shape
    total_rows = flat // heads_each
    block_len = own_ref.shape[0]
    me = lax.axis_index("ctx")
    limits = limit_ref[...][:, 0:1]
    query, rope_query = query_ref[...], rope_query_ref[...]
    core = lax.rem(me, 2)
    owners = [me, lax.bitwise_xor(me, 1), lax.bitwise_xor(me, 2 + 2 * core), lax.bitwise_xor(me, 5 - 2 * core)]
    highest = jnp.maximum(
        jnp.max(scores_ref[0], axis=1, keepdims=True), jnp.max(scores_ref[1], axis=1, keepdims=True)
    )
    for index, (block, rope_block) in enumerate(((near_ref, near_rope_ref), (far_ref, far_rope_ref))):
        begin = owners[index + 2] * block_len
        scores = score_block(query, rope_query, block[...], rope_block[...], begin, limits, heads_each)
        more_ref[index] = scores
        highest = jnp.maximum(highest, jnp.max(scores, axis=1, keepdims=True))
    highest = jnp.maximum(highest, no_position)
    total = None
    summed = None
    for index, block in enumerate((own_ref, core_ref, near_ref, far_ref)):
        scores = scores_ref[index] if index < 2 else more_ref[index - 2]
        weights = jnp.exp2((scores - highest) * exponent_scale).astype(bf16)
        part = jnp.sum(weights.astype(f32), axis=1, keepdims=True)
        summed = part if summed is None else summed + part
        part = jnp.dot(weights, block[...], preferred_element_type=f32)
        total = part if total is None else total + part
    lane = lax.broadcasted_iota(jnp.int32, (8, 128), 1)
    for head in range(heads_each):
        base = head * total_rows
        out_ref[head, 0:total_rows, :] = total[base : base + total_rows].astype(bf16)
        note = jnp.zeros((8, 128), f32)
        for tile in range(total_rows // 8):
            for offset, value in ((0, highest), (3, summed)):
                value = jnp.broadcast_to(value[base + tile * 8 : base + tile * 8 + 8], (8, 128))
                for piece in range(3):
                    rounded = value.astype(bf16).astype(f32)
                    note = jnp.where(lane == 8 * tile + offset + piece, rounded, note)
                    value = value - rounded
        wide = jnp.concatenate([note, jnp.zeros((8, out_ref.shape[2] - 128), f32)], axis=1)
        out_ref[head, total_rows:, :] = wide.astype(bf16)


def merge_project(arrived_ref, weight_ref, own_ref, other_ref, attention_ref, product_ref):
    sources, height, _ = arrived_ref.shape
    total_rows = height - 8
    peaks = []
    sums = []
    for source in range(sources):
        note = arrived_ref[source, total_rows:, 0:128].astype(f32)
        shifted = [note] + [pltpu.roll(note, 128 - step, 1) for step in range(1, 6)]
        peaks.append(shifted[0] + shifted[1] + shifted[2])
        sums.append(shifted[3] + shifted[4] + shifted[5])
    highest = functools.reduce(jnp.maximum, peaks)
    factors = [jnp.exp2((peak - highest) * exponent_scale) for peak in peaks]
    divisor = sum(factor * part for factor, part in zip(factors, sums))
    factors = [factor / divisor for factor in factors]
    for tile in range(total_rows // 8):
        span = slice(tile * 8, tile * 8 + 8)
        attention_ref[span, :] = sum(
            factor[:, 8 * tile : 8 * tile + 1] * arrived_ref[source, span, :].astype(f32)
            for source, factor in enumerate(factors)
        )
    product = jnp.dot(attention_ref[...].astype(bf16), weight_ref[...], preferred_element_type=f32)
    product_ref[...] = product.reshape(product_ref.shape)
    core = lax.rem(lax.axis_index("ctx"), 2)
    own_ref[...] = product_ref[core]
    other_ref[...] = product_ref[1 - core].astype(bf16)


def strips_of(array):
    return jnp.concatenate(
        [array[:, part * strip : (part + 1) * strip] for part in range(array.shape[1] // strip)], axis=0
    )


def combine(own_ref, other_ref, order_ref, out_ref):
    summed = strips_of(own_ref[...] + other_ref[...].astype(f32)).astype(bf16)
    ordered = jnp.dot(order_ref[...], summed, preferred_element_type=f32).astype(bf16)
    out_ref[...] = ordered.reshape(out_ref.shape)


def norm_rows(arrived_ref, residual_ref, gain_ref, projected_ref, hidden_ref, out_ref, natural, stripped):
    rows, width = residual_ref.shape
    strips = width // strip
    summed = jnp.sum(arrived_ref[...].astype(f32), axis=0)
    for row in range(rows):
        for part in range(strips):
            at = row * strips + part
            natural[row : row + 1, part * strip : (part + 1) * strip] = summed[at : at + 1]
    projected = natural[0:rows, :]
    projected_ref[...] = projected
    hidden = residual_ref[...].astype(f32) + projected
    hidden_ref[...] = hidden
    scale = lax.rsqrt(jnp.mean(hidden * hidden, axis=1, keepdims=True) + norm_eps)
    normed = hidden * scale * gain_ref[...].reshape(1, width)
    stripped[...] = jnp.zeros_like(stripped)
    for row in range(rows):
        for part in range(strips):
            at = row * strips + part
            stripped[at : at + 1, :] = normed[row : row + 1, part * strip : (part + 1) * strip]
    tile = stripped[...].astype(bf16)
    for chip in range(out_ref.shape[0]):
        out_ref[chip] = tile


def run_expert(rows, own_rows_ref, other_rows_ref, back_ref, ids_ref, route_ref, gate_ref, up_ref, down_ref, own_ref, other_ref):
    chips, height, _ = own_rows_ref.shape
    half_rows = chips * rows
    strips = gate_ref.shape[0] // strip
    me = lax.axis_index("ctx")
    ordered = [
        jnp.dot(back_ref[...], ref[...].reshape(chips * height, strip), preferred_element_type=f32)
        for ref in (own_rows_ref, other_rows_ref)
    ]
    inputs = jnp.concatenate(
        [
            jnp.concatenate([part[at * half_rows : (at + 1) * half_rows] for part in ordered], axis=0)
            for at in range(strips)
        ],
        axis=1,
    ).astype(bf16)
    row = lax.broadcasted_iota(jnp.int32, (1, 2 * half_rows), 1)
    device = sum((row >= step * rows).astype(jnp.int32) for step in range(1, 2 * chips))
    other = (lax.rem(device, 2) != lax.rem(me, 2)).astype(jnp.int32)
    target = other * half_rows + lax.shift_right_logical(device, 1) * rows + row - device * rows
    named = jnp.sum(jnp.where(ids_ref[...] == me, route_ref[...], 0.0), axis=0, keepdims=True)
    place = lax.broadcasted_iota(jnp.int32, (2 * half_rows, 2 * half_rows), 0)
    weight = jnp.sum(jnp.where(place == target, named, 0.0), axis=1, keepdims=True)
    gate = jnp.dot(inputs, gate_ref[...], preferred_element_type=f32)
    up = jnp.dot(inputs, up_ref[...], preferred_element_type=f32)
    hidden = (gate * (1.0 / (1.0 + jnp.exp(-gate))) * up).astype(bf16)
    result = jnp.dot(hidden, down_ref[...], preferred_element_type=f32)
    result = jnp.where(weight > 0.0, result * weight, 0.0)
    own_ref[...] = result[:half_rows]
    other_ref[...] = result[half_rows:].astype(bf16)


def add_mixture(arrived_ref, hidden_ref, projected_ref, attn_ref, out_ref, natural):
    rows, width = hidden_ref.shape
    strips = width // strip
    attn_ref[...] = projected_ref[...].astype(bf16)
    mixture = jnp.sum(arrived_ref[...].astype(f32), axis=0)
    for row in range(rows):
        for part in range(strips):
            at = row * strips + part
            natural[row : row + 1, part * strip : (part + 1) * strip] = mixture[at : at + 1]
    out_ref[...] = (hidden_ref[...] + natural[0:rows, :]).astype(bf16)


def kernel_layer(
    query_latent,
    query_rope,
    cache_latent,
    cache_rope,
    valid_len,
    w_vo,
    residual,
    norm_gain,
    expert_ids,
    route_weight,
    w_gate,
    w_up,
    w_down,
):
    devices = lax.axis_size("ctx")
    rows, width = residual.shape
    block_len, latent = cache_latent.shape
    rope_dim = cache_rope.shape[0]
    head_count = query_rope.shape[1] // rope_dim
    total_rows = rows * devices
    heads_each = head_count // share
    per = rows * heads_each
    strips = width // strip
    height = 8 * -(-rows * strips // 8)

    def swap(array):
        return lax.ppermute(array, "ctx", [(d, d ^ 1) for d in range(devices)])

    def trade(array):
        return lax.ppermute(array, "ctx", [(d, d ^ (2 + d % 2 * 2)) for d in range(devices)])

    tiles = 2 * per // 8 * 2 + 1
    flat = heads_each * total_rows
    outgoing = call(
        functools.partial(prepare, heads_each),
        jax.ShapeDtypeStruct((devices, tiles, 8, 128), bf16),
        query_latent,
        query_rope,
        spaces={0: pltpu.HBM, 1: pltpu.HBM},
        limit=60,
        scratch=[
            VMEM(query_latent.shape, bf16),
            VMEM(query_rope.shape, bf16),
            VMEM((share, 2 * per, latent // 2), f32),
            VMEM((share, 16, 128), f32),
            VMEM((share, tiles, 8, 128), bf16),
            pltpu.SemaphoreType.DMA((2,)),
            pltpu.SemaphoreType.DMA((devices,)),
        ],
        out_space=pl.ANY,
    )
    near = trade(cache_latent)
    rope, outgoing = lax.optimization_barrier((cache_rope, outgoing))
    core = swap(cache_latent)
    core_rope = swap(rope)
    near_rope = trade(rope)
    arrived = lax.all_to_all(outgoing, "ctx", split_axis=0, concat_axis=0, tiled=True)
    order, rope_order, limits = call(
        functools.partial(tables, rows, heads_each),
        (
            jax.ShapeDtypeStruct((2 * flat, 2 * per // 8 * devices * 8), bf16),
            jax.ShapeDtypeStruct((2 * flat, devices * 8), bf16),
            jax.ShapeDtypeStruct((total_rows, 128), jnp.int32),
        ),
        valid_len,
        spaces={0: SMEM},
    )
    far_rope = swap(near_rope)
    near, core, core_rope, far_rope, order, rope_order, limits, arrived = lax.optimization_barrier(
        (near, core, core_rope, far_rope, order, rope_order, limits, arrived)
    )
    far = swap(near)
    query, rope_query, scores = call(
        functools.partial(score_near, heads_each),
        (
            jax.ShapeDtypeStruct((flat, latent), bf16),
            jax.ShapeDtypeStruct((flat, 256), bf16),
            jax.ShapeDtypeStruct((2, flat, block_len), f32),
        ),
        arrived,
        order,
        rope_order,
        limits,
        cache_latent,
        cache_rope,
        core,
        core_rope,
    )
    partial = call(
        functools.partial(attend, heads_each),
        jax.ShapeDtypeStruct((heads_each, total_rows + 8, latent), bf16),
        query,
        rope_query,
        scores,
        limits,
        cache_latent,
        core,
        near,
        far,
        near_rope,
        far_rope,
        scratch=[VMEM((2, flat, block_len), f32)],
    )
    lines = [[d for d in range(devices) if place(d) == kind] for kind in range(share)]
    chips = devices // 2
    half_rows = rows * chips
    same_core = [[2 * chip + c for chip in range(chips)] for c in range(2)]
    send = strip_order(rows, chips, strips, height)
    send_order, back_order = jnp.asarray(send, bf16), jnp.asarray(send.T, bf16)
    strip_shape = jax.ShapeDtypeStruct((chips, height, strip), bf16)
    halves = (
        jax.ShapeDtypeStruct((half_rows, width), f32),
        jax.ShapeDtypeStruct((half_rows, width), bf16),
    )

    def exchange(array, partners):
        return lax.all_to_all(array, "ctx", split_axis=0, concat_axis=0, axis_index_groups=partners, tiled=True)

    pieces = exchange(partial, lines)
    kept, given = call(
        merge_project,
        halves,
        pieces,
        w_vo,
        scratch=[VMEM((total_rows, latent), f32), VMEM((2, half_rows, width), f32)],
    )
    columns = call(combine, strip_shape, kept, swap(given), send_order)
    projected, hidden_state, normed = call(
        norm_rows,
        (
            jax.ShapeDtypeStruct((rows, width), f32),
            jax.ShapeDtypeStruct((rows, width), f32),
            strip_shape,
        ),
        exchange(columns, same_core),
        residual,
        norm_gain,
        scratch=[VMEM((8, width), f32), VMEM((height, strip), f32)],
    )
    inputs = exchange(normed, same_core)
    kept, given = call(
        functools.partial(run_expert, rows),
        halves,
        inputs,
        swap(inputs),
        back_order,
        expert_ids.T,
        route_weight.T,
        w_gate[0],
        w_up[0],
        w_down[0],
    )
    results = call(combine, strip_shape, kept, swap(given), send_order)
    attn_out, layer_out = call(
        add_mixture,
        (jax.ShapeDtypeStruct((rows, width), bf16), jax.ShapeDtypeStruct((rows, width), bf16)),
        exchange(results, same_core),
        hidden_state,
        projected,
        scratch=[VMEM((8, width), f32)],
    )
    return attn_out, layer_out


def fits(mesh, query_rope, residual, cache_latent, cache_rope):
    devices = mesh.shape["ctx"]
    rope_dim = cache_rope.shape[0] // mesh.shape["groups"]
    heads = query_rope.shape[1] // rope_dim
    rows = residual.shape[0] // (devices * mesh.shape["groups"])
    per = rows * heads // share
    return (
        heads == devices
        and devices % (2 * share) == 0
        and rope_dim == 64
        and 2 * per % 8 == 0
        and 8 <= per <= 16
        and rows * devices % 16 == 0
        and rows * devices <= 128
        and cache_latent.shape[1] == 512
        and cache_latent.shape[0] // (devices * mesh.shape["groups"]) == 512
        and devices & (devices - 1) == 0
        and residual.shape[1] % strip == 0
    )


def solution(mesh):
    in_specs = (
        P(("groups", "ctx"), None),
        P(("groups", "ctx"), None),
        P(("groups", "ctx"), None),
        P("groups", "ctx"),
        P("groups"),
        P("ctx", None),
        P(("groups", "ctx"), None),
        P(),
        P("groups", None),
        P("groups", None),
        P("ctx", None, None),
        P("ctx", None, None),
        P("ctx", None, None),
    )
    out_specs = (P(("groups", "ctx"), None), P(("groups", "ctx"), None))

    def layer(*args):
        kernels = fits(mesh, args[1], args[6], args[2], args[3])

        def body(*shards):
            return (kernel_layer if kernels else plain_layer)(*shards)

        step = jax.shard_map(body, mesh=mesh, in_specs=in_specs, out_specs=out_specs, check_vma=False)
        return step(*args)

    return layer
```

```python
import functools
import math

import jax
import jax.numpy as jnp
import numpy as np
from jax import lax
from jax.experimental import pallas as pl
from jax.experimental.pallas import tpu as pltpu
from jax.sharding import PartitionSpec as P


softmax_scale = 192.0 ** (-0.5)
negative_fill = -1e30
norm_eps = 1e-06
exponent_scale = softmax_scale * math.log2(math.e)
no_position = -1e29
share = 4
strip = 512

VMEM = pltpu.VMEM
SMEM = pltpu.SMEM
f32 = jnp.float32
bf16 = jnp.bfloat16


def expert_apply(inputs, gate_weight, up_weight, down_weight):
    gate_out = jnp.dot(inputs, gate_weight, preferred_element_type=jnp.float32)
    up_out = jnp.dot(inputs, up_weight, preferred_element_type=jnp.float32)
    hidden = (jax.nn.silu(gate_out) * up_out).astype(jnp.bfloat16)
    return jnp.dot(hidden, down_weight, preferred_element_type=jnp.float32).astype(jnp.bfloat16)


def plain_layer(
    query_latent,
    query_rope,
    cache_latent,
    cache_rope,
    valid_len,
    w_vo,
    residual,
    norm_gain,
    expert_ids,
    route_weight,
    w_gate,
    w_up,
    w_down,
):
    query_all, rope_all = (
        lax.all_gather(query_latent, "ctx", axis=0, tiled=True),
        lax.all_gather(query_rope, "ctx", axis=0, tiled=True),
    )
    total_rows = query_all.shape[0]
    own_rows = residual.shape[0]
    latent = cache_latent.shape[1]
    rope_dim = cache_rope.shape[0]
    head_count = rope_all.shape[1] // rope_dim
    block_len = cache_latent.shape[0]
    devices = lax.axis_size("ctx")
    self_index = lax.axis_index("ctx")
    col_count = head_count * latent // devices
    flat_query = query_all.reshape(total_rows * head_count, latent)
    flat_rope = rope_all.reshape(total_rows * head_count, rope_dim)
    scores = lax.dot_general(
        flat_query, cache_latent, (((1,), (1,)), ((), ())), preferred_element_type=jnp.float32
    )
    scores = (
        scores + jnp.dot(flat_rope, cache_rope, preferred_element_type=jnp.float32)
    ) * softmax_scale
    position = self_index * block_len + lax.broadcasted_iota(jnp.int32, (1, block_len), 1)
    usable = position < jnp.repeat(valid_len, head_count)[:, None]
    block_max = jnp.max(jnp.where(usable, scores, negative_fill), axis=1)
    weights = jnp.where(usable, jnp.exp(scores - block_max[:, None]), 0.0).astype(jnp.bfloat16)
    block_sum = jnp.sum(weights.astype(jnp.float32), axis=1)
    block_out = jnp.dot(weights, cache_latent, preferred_element_type=jnp.float32)
    row_max = block_max.reshape(total_rows, head_count)
    row_sum = block_sum.reshape(total_rows, head_count)
    global_max = lax.pmax(row_max, "ctx")
    factor = jnp.exp(row_max - global_max)
    scaled = (block_out.reshape(total_rows, head_count, latent) * factor[:, :, None]).reshape(
        total_rows, head_count * latent
    )
    merged = lax.psum_scatter(scaled, "ctx", scatter_dimension=1, tiled=True)
    totals = lax.psum(row_sum * factor, "ctx")
    divisor = lax.dynamic_slice_in_dim(totals, self_index * col_count // latent, 1, 1)
    attention = (merged / divisor).astype(jnp.bfloat16)
    projected = lax.psum_scatter(
        jnp.dot(attention, w_vo, preferred_element_type=jnp.float32),
        "ctx",
        scatter_dimension=0,
        tiled=True,
    )
    hidden_state = residual.astype(jnp.float32) + projected
    normed = (
        hidden_state
        * lax.rsqrt(jnp.mean(hidden_state * hidden_state, axis=1, keepdims=True) + norm_eps)
        * norm_gain
    ).astype(jnp.bfloat16)
    expert_iota = lax.broadcasted_iota(jnp.int32, (1, 1, devices), 2)
    route_table = jnp.sum(
        jnp.where(expert_ids[:, :, None] == expert_iota, route_weight[:, :, None], 0.0), axis=1
    )
    gate_own = w_gate[0]
    up_own = w_up[0]
    down_own = w_down[0]
    own_table = jnp.transpose(
        lax.dynamic_slice_in_dim(route_table, self_index * own_rows, own_rows, 0)
    )
    outgoing = jnp.where(
        own_table[:, :, None] > 0.0, normed[None, :, :], jnp.zeros((), jnp.bfloat16)
    )
    arrived = lax.all_to_all(outgoing, "ctx", split_axis=0, concat_axis=0, tiled=True)
    item_count = arrived.shape[1]
    stacked = arrived.reshape(devices * item_count, arrived.shape[2])
    result = expert_apply(stacked, gate_own, up_own, down_own).reshape(
        devices, item_count, arrived.shape[2]
    )
    returned = lax.all_to_all(result, "ctx", split_axis=0, concat_axis=0, tiled=True)
    mixture = jnp.sum(own_table[:, :, None] * returned.astype(jnp.float32), axis=0)
    layer_out = (hidden_state + mixture).astype(jnp.bfloat16)
    return (projected.astype(jnp.bfloat16), layer_out)


def place(device):
    return 2 * ((device // 2 ^ device // 4) & 1) + device % 2


def call(kernel, out_shape, *operands, spaces=None, scratch=(), limit=24, out_space=VMEM):
    spaces = spaces or {}
    in_specs = [pl.BlockSpec(memory_space=spaces.get(i, VMEM)) for i in range(len(operands))]
    many = isinstance(out_shape, (tuple, list))
    out_specs = [pl.BlockSpec(memory_space=VMEM) for _ in out_shape] if many else pl.BlockSpec(memory_space=out_space)
    return pl.pallas_call(
        kernel,
        out_shape=out_shape,
        in_specs=in_specs,
        out_specs=out_specs,
        scratch_shapes=list(scratch),
        compiler_params=pltpu.CompilerParams(vmem_limit_bytes=limit << 20),
        cost_estimate=pl.CostEstimate(flops=4 * 10**9, bytes_accessed=64 << 20, transcendentals=0),
    )(*operands)


def strip_order(rows, devices, strips, height):
    order = np.zeros((devices * height, strips * rows * devices), np.float32)
    for device in range(devices):
        for row in range(rows):
            for part in range(strips):
                order[device * height + row * strips + part, part * rows * devices + device * rows + row] = 1.0
    return order


def prepare(heads_each, query_hbm, rope_hbm, out_ref, query_ref, rope_ref, piece, rope_piece, arrive):
    copies = [
        pltpu.make_async_copy(query_hbm, query_ref, arrive.at[0]),
        pltpu.make_async_copy(rope_hbm, rope_ref, arrive.at[1]),
    ]
    for copy in copies:
        copy.start()
    rows = query_ref.shape[0]
    per = rows * heads_each
    latent = query_ref.shape[1] // (heads_each * share)
    rope_dim = rope_ref.shape[1] // (heads_each * share)
    half_width = latent // 2
    devices = out_ref.shape[0]
    lane = lax.broadcasted_iota(jnp.int32, (8, 128), 1)
    rope_piece[...] = jnp.zeros_like(rope_piece)
    for copy in copies:
        copy.wait()
    query = query_ref[...].astype(f32)
    rope = rope_ref[...].astype(f32)
    for kind in range(share):
        owners = [device for device in range(devices) if place(device) == kind]
        for item in range(per):
            row, index = divmod(item, heads_each)
            head = owners[index]
            for half in range(2):
                begin = head * latent + half * half_width
                piece[kind, half * per + item : half * per + item + 1, :] = query[row : row + 1, begin : begin + half_width]
            block = head * rope_dim // 128
            rope_piece[kind, item : item + 1, :] = rope[row : row + 1, block * 128 : (block + 1) * 128]
    for kind in range(share):
        first = rope_piece[kind, 0:8, :]
        second = rope_piece[kind, 8:16, :]
        if kind % 2 == 1:
            first = pltpu.roll(first, 64, 1)
        else:
            second = pltpu.roll(second, 64, 1)
        tail = jnp.where(lane < 64, first, second).astype(bf16)
        tiles = []
        for rt in range(2 * per // 8):
            for lt in range(half_width // 128):
                tiles.append(piece[kind, rt * 8 : (rt + 1) * 8, lt * 128 : (lt + 1) * 128].astype(bf16))
        tiles.append(tail)
        for device in range(devices):
            if place(device) == kind:
                for index, tile in enumerate(tiles):
                    out_ref[device, index] = tile


def place_of(item, source, rows, heads_each, total_rows):
    row = sum((item >= step * heads_each).astype(jnp.int32) for step in range(1, rows))
    head = item - row * heads_each
    core, chip = lax.rem(source, 2), lax.shift_right_logical(source, 1)
    return head * total_rows + core * (total_rows // 2) + chip * rows + row


def one_hot(target, height):
    return (lax.broadcasted_iota(jnp.int32, (height, target.shape[1]), 0) == target).astype(f32).astype(bf16)


def tables(rows, heads_each, length_ref, order_ref, rope_order_ref, limit_ref):
    total_rows = limit_ref.shape[0]
    devices = total_rows // rows
    flat = heads_each * total_rows
    per = rows * heads_each
    for row in range(total_rows):
        device, index = divmod(row, rows)
        at = device % 2 * (total_rows // 2) + device // 2 * rows + index
        limit_ref[at : at + 1, :] = jnp.full((1, 128), length_ref[row], jnp.int32)
    column = lax.broadcasted_iota(jnp.int32, (1, order_ref.shape[1]), 1)
    source = lax.rem(lax.shift_right_logical(column, 3), devices)
    unit = lax.div(column, devices * 8) * 8 + lax.rem(column, 8)
    second = (unit >= per).astype(jnp.int32)
    target = second * flat + place_of(unit - second * per, source, rows, heads_each, total_rows)
    order_ref[...] = one_hot(target, 2 * flat)
    column = lax.broadcasted_iota(jnp.int32, (1, devices * 8), 1)
    source = lax.shift_right_logical(column, 3)
    item = lax.rem(column, 8)
    for half in range(2):
        shifted = item + 8 * half
        target = jnp.where(shifted < per, place_of(shifted, source, rows, heads_each, total_rows), -1)
        rope_order_ref[half * flat : (half + 1) * flat, :] = one_hot(target, flat)


def score_block(query, rope_query, block_ref, rope_block_ref, owner, limits, heads_each):
    flat = query.shape[0]
    total_rows = flat // heads_each
    width = rope_block_ref.shape[1]
    rope_keys = rope_block_ref[...]
    empty = jnp.zeros_like(rope_keys)
    rope_keys = jnp.concatenate([rope_keys, empty, empty, rope_keys], axis=0)
    scores = lax.dot_general(query, block_ref[...], (((1,), (1,)), ((), ())), preferred_element_type=f32)
    scores = scores + jnp.dot(rope_query, rope_keys, preferred_element_type=f32)
    valid = lax.broadcasted_iota(jnp.int32, (total_rows, width), 1) + owner * width < limits
    return jnp.where(valid[None], scores.reshape(heads_each, total_rows, width), negative_fill).reshape(flat, width)


def weigh(scores, highest, block_ref):
    weights = jnp.exp2((scores - highest) * exponent_scale).astype(bf16)
    summed = jnp.sum(weights.astype(f32), axis=1, keepdims=True)
    return summed, jnp.dot(weights, block_ref[...], preferred_element_type=f32)


def attend_three(heads_each, arrived_ref, order_ref, rope_order_ref, limit_ref, own_ref, own_rope_ref, core_ref, core_rope_ref, near_ref, near_rope_ref, query_ref, rope_query_ref, state_ref, total_ref, scores_ref):
    devices = arrived_ref.shape[0]
    flat = order_ref.shape[0] // 2
    row_tiles = arrived_ref.shape[1] // 2
    me = lax.axis_index("ctx")
    gathered = jnp.concatenate(
        [
            jnp.concatenate(
                [arrived_ref[:, 2 * rt + lt].reshape(devices * 8, 128) for lt in range(2)], axis=1
            )
            for rt in range(row_tiles)
        ],
        axis=0,
    )
    ordered = jnp.dot(order_ref[...], gathered, preferred_element_type=f32).astype(bf16)
    query = jnp.concatenate([ordered[:flat], ordered[flat:]], axis=1)
    rope_rows = arrived_ref[:, 2 * row_tiles].reshape(devices * 8, 128)
    ordered = jnp.dot(rope_order_ref[...], rope_rows, preferred_element_type=f32).astype(bf16)
    rope_query = jnp.concatenate([ordered[:flat], ordered[flat:]], axis=1)
    query_ref[...] = query
    rope_query_ref[...] = rope_query
    limits = limit_ref[...][:, 0:1]
    blocks = (own_ref, core_ref, near_ref)
    rope_blocks = (own_rope_ref, core_rope_ref, near_rope_ref)
    owners = (me, lax.bitwise_xor(me, 1), lax.bitwise_xor(me, 2 + 2 * lax.rem(me, 2)))
    highest = jnp.full((flat, 1), no_position, f32)
    for index, (block, rope_block, owner) in enumerate(zip(blocks, rope_blocks, owners)):
        scores = score_block(query, rope_query, block, rope_block, owner, limits, heads_each)
        scores_ref[index] = scores
        highest = jnp.maximum(highest, jnp.max(scores, axis=1, keepdims=True))
    parts = [weigh(scores_ref[index], highest, block) for index, block in enumerate(blocks)]
    state_ref[0] = jnp.broadcast_to(highest, state_ref.shape[1:])
    state_ref[1] = jnp.broadcast_to(sum(part[0] for part in parts), state_ref.shape[1:])
    total_ref[...] = sum(part[1] for part in parts)


def attend_last(heads_each, query_ref, rope_query_ref, state_ref, total_ref, limit_ref, far_ref, far_rope_ref, out_ref):
    flat, _ = query_ref.shape
    total_rows = flat // heads_each
    me = lax.axis_index("ctx")
    owner = lax.bitwise_xor(me, 5 - 2 * lax.rem(me, 2))
    limits = limit_ref[...][:, 0:1]
    scores = score_block(query_ref[...], rope_query_ref[...], far_ref, far_rope_ref, owner, limits, heads_each)
    before = state_ref[0][:, 0:1]
    highest = jnp.maximum(before, jnp.max(scores, axis=1, keepdims=True))
    kept = jnp.exp2((before - highest) * exponent_scale)
    summed, total = weigh(scores, highest, far_ref)
    summed = summed + kept * state_ref[1][:, 0:1]
    total = total + kept * total_ref[...]
    lane = lax.broadcasted_iota(jnp.int32, (8, 128), 1)
    for head in range(heads_each):
        base = head * total_rows
        out_ref[head, 0:total_rows, :] = total[base : base + total_rows].astype(bf16)
        note = jnp.zeros((8, 128), f32)
        for tile in range(total_rows // 8):
            for offset, value in ((0, highest), (3, summed)):
                value = jnp.broadcast_to(value[base + tile * 8 : base + tile * 8 + 8], (8, 128))
                for piece in range(3):
                    rounded = value.astype(bf16).astype(f32)
                    note = jnp.where(lane == 8 * tile + offset + piece, rounded, note)
                    value = value - rounded
        wide = jnp.concatenate([note, jnp.zeros((8, out_ref.shape[2] - 128), f32)], axis=1)
        out_ref[head, total_rows:, :] = wide.astype(bf16)


def merge_project(arrived_ref, weight_ref, own_ref, other_ref, attention_ref, product_ref):
    sources, height, _ = arrived_ref.shape
    total_rows = height - 8
    peaks = []
    sums = []
    for source in range(sources):
        note = arrived_ref[source, total_rows:, 0:128].astype(f32)
        shifted = [note] + [pltpu.roll(note, 128 - step, 1) for step in range(1, 6)]
        peaks.append(shifted[0] + shifted[1] + shifted[2])
        sums.append(shifted[3] + shifted[4] + shifted[5])
    highest = functools.reduce(jnp.maximum, peaks)
    factors = [jnp.exp2((peak - highest) * exponent_scale) for peak in peaks]
    divisor = sum(factor * part for factor, part in zip(factors, sums))
    factors = [factor / divisor for factor in factors]
    for tile in range(total_rows // 8):
        span = slice(tile * 8, tile * 8 + 8)
        attention_ref[span, :] = sum(
            factor[:, 8 * tile : 8 * tile + 1] * arrived_ref[source, span, :].astype(f32)
            for source, factor in enumerate(factors)
        )
    product = jnp.dot(attention_ref[...].astype(bf16), weight_ref[...], preferred_element_type=f32)
    product_ref[...] = product.reshape(product_ref.shape)
    core = lax.rem(lax.axis_index("ctx"), 2)
    own_ref[...] = product_ref[core]
    other_ref[...] = product_ref[1 - core].astype(bf16)


def strips_of(array):
    return jnp.concatenate(
        [array[:, part * strip : (part + 1) * strip] for part in range(array.shape[1] // strip)], axis=0
    )


def combine(own_ref, other_ref, order_ref, out_ref):
    summed = strips_of(own_ref[...] + other_ref[...].astype(f32)).astype(bf16)
    ordered = jnp.dot(order_ref[...], summed, preferred_element_type=f32).astype(bf16)
    out_ref[...] = ordered.reshape(out_ref.shape)


def norm_rows(arrived_ref, residual_ref, gain_ref, projected_ref, hidden_ref, out_ref, natural, stripped):
    rows, width = residual_ref.shape
    strips = width // strip
    summed = jnp.sum(arrived_ref[...].astype(f32), axis=0)
    for row in range(rows):
        for part in range(strips):
            at = row * strips + part
            natural[row : row + 1, part * strip : (part + 1) * strip] = summed[at : at + 1]
    projected = natural[0:rows, :]
    projected_ref[...] = projected
    hidden = residual_ref[...].astype(f32) + projected
    hidden_ref[...] = hidden
    scale = lax.rsqrt(jnp.mean(hidden * hidden, axis=1, keepdims=True) + norm_eps)
    normed = hidden * scale * gain_ref[...].reshape(1, width)
    stripped[...] = jnp.zeros_like(stripped)
    for row in range(rows):
        for part in range(strips):
            at = row * strips + part
            stripped[at : at + 1, :] = normed[row : row + 1, part * strip : (part + 1) * strip]
    tile = stripped[...].astype(bf16)
    for chip in range(out_ref.shape[0]):
        out_ref[chip] = tile


def run_expert(rows, own_rows_ref, other_rows_ref, back_ref, ids_ref, route_ref, gate_ref, up_ref, down_ref, own_ref, other_ref):
    chips, height, _ = own_rows_ref.shape
    half_rows = chips * rows
    strips = gate_ref.shape[0] // strip
    me = lax.axis_index("ctx")
    ordered = [
        jnp.dot(back_ref[...], ref[...].reshape(chips * height, strip), preferred_element_type=f32)
        for ref in (own_rows_ref, other_rows_ref)
    ]
    inputs = jnp.concatenate(
        [
            jnp.concatenate([part[at * half_rows : (at + 1) * half_rows] for part in ordered], axis=0)
            for at in range(strips)
        ],
        axis=1,
    ).astype(bf16)
    row = lax.broadcasted_iota(jnp.int32, (1, 2 * half_rows), 1)
    device = sum((row >= step * rows).astype(jnp.int32) for step in range(1, 2 * chips))
    other = (lax.rem(device, 2) != lax.rem(me, 2)).astype(jnp.int32)
    target = other * half_rows + lax.shift_right_logical(device, 1) * rows + row - device * rows
    named = jnp.sum(jnp.where(ids_ref[...] == me, route_ref[...], 0.0), axis=0, keepdims=True)
    place = lax.broadcasted_iota(jnp.int32, (2 * half_rows, 2 * half_rows), 0)
    weight = jnp.sum(jnp.where(place == target, named, 0.0), axis=1, keepdims=True)
    gate = jnp.dot(inputs, gate_ref[...], preferred_element_type=f32)
    up = jnp.dot(inputs, up_ref[...], preferred_element_type=f32)
    hidden = (gate * (1.0 / (1.0 + jnp.exp(-gate))) * up).astype(bf16)
    result = jnp.dot(hidden, down_ref[...], preferred_element_type=f32)
    result = jnp.where(weight > 0.0, result * weight, 0.0)
    own_ref[...] = result[:half_rows]
    other_ref[...] = result[half_rows:].astype(bf16)


def add_mixture(arrived_ref, hidden_ref, projected_ref, attn_ref, out_ref, natural):
    rows, width = hidden_ref.shape
    strips = width // strip
    attn_ref[...] = projected_ref[...].astype(bf16)
    mixture = jnp.sum(arrived_ref[...].astype(f32), axis=0)
    for row in range(rows):
        for part in range(strips):
            at = row * strips + part
            natural[row : row + 1, part * strip : (part + 1) * strip] = mixture[at : at + 1]
    out_ref[...] = (hidden_ref[...] + natural[0:rows, :]).astype(bf16)


def kernel_layer(
    query_latent,
    query_rope,
    cache_latent,
    cache_rope,
    valid_len,
    w_vo,
    residual,
    norm_gain,
    expert_ids,
    route_weight,
    w_gate,
    w_up,
    w_down,
):
    devices = lax.axis_size("ctx")
    rows, width = residual.shape
    block_len, latent = cache_latent.shape
    rope_dim = cache_rope.shape[0]
    head_count = query_rope.shape[1] // rope_dim
    total_rows = rows * devices
    heads_each = head_count // share
    per = rows * heads_each
    strips = width // strip
    height = 8 * -(-rows * strips // 8)

    def swap(array):
        return lax.ppermute(array, "ctx", [(d, d ^ 1) for d in range(devices)])

    def trade(array):
        return lax.ppermute(array, "ctx", [(d, d ^ (2 + d % 2 * 2)) for d in range(devices)])

    tiles = 2 * per // 8 * 2 + 1
    flat = heads_each * total_rows
    outgoing = call(
        functools.partial(prepare, heads_each),
        jax.ShapeDtypeStruct((devices, tiles, 8, 128), bf16),
        query_latent,
        query_rope,
        spaces={0: pltpu.HBM, 1: pltpu.HBM},
        limit=60,
        scratch=[
            VMEM(query_latent.shape, bf16),
            VMEM(query_rope.shape, bf16),
            VMEM((share, 2 * per, latent // 2), f32),
            VMEM((share, 16, 128), f32),
            pltpu.SemaphoreType.DMA((2,)),
        ],
    )
    near = trade(cache_latent)
    rope, outgoing = lax.optimization_barrier((cache_rope, outgoing))
    core = swap(cache_latent)
    core_rope = swap(rope)
    near_rope = trade(rope)
    arrived = lax.all_to_all(outgoing, "ctx", split_axis=0, concat_axis=0, tiled=True)
    order, rope_order, limits = call(
        functools.partial(tables, rows, heads_each),
        (
            jax.ShapeDtypeStruct((2 * flat, 2 * per // 8 * devices * 8), bf16),
            jax.ShapeDtypeStruct((2 * flat, devices * 8), bf16),
            jax.ShapeDtypeStruct((total_rows, 128), jnp.int32),
        ),
        valid_len,
        spaces={0: SMEM},
    )
    near, near_rope, core, core_rope, order, rope_order, limits, arrived = lax.optimization_barrier(
        (near, near_rope, core, core_rope, order, rope_order, limits, arrived)
    )
    far, far_rope = swap(near), swap(near_rope)
    query, rope_query, state, total = call(
        functools.partial(attend_three, heads_each),
        (
            jax.ShapeDtypeStruct((flat, latent), bf16),
            jax.ShapeDtypeStruct((flat, 256), bf16),
            jax.ShapeDtypeStruct((2, flat, 128), f32),
            jax.ShapeDtypeStruct((flat, latent), f32),
        ),
        arrived,
        order,
        rope_order,
        limits,
        cache_latent,
        cache_rope,
        core,
        core_rope,
        near,
        near_rope,
        scratch=[VMEM((3, flat, block_len), f32)],
    )
    partial = call(
        functools.partial(attend_last, heads_each),
        jax.ShapeDtypeStruct((heads_each, total_rows + 8, latent), bf16),
        query,
        rope_query,
        state,
        total,
        limits,
        far,
        far_rope,
    )
    lines = [[d for d in range(devices) if place(d) == kind] for kind in range(share)]
    chips = devices // 2
    half_rows = rows * chips
    same_core = [[2 * chip + c for chip in range(chips)] for c in range(2)]
    send = strip_order(rows, chips, strips, height)
    send_order, back_order = jnp.asarray(send, bf16), jnp.asarray(send.T, bf16)
    strip_shape = jax.ShapeDtypeStruct((chips, height, strip), bf16)
    halves = (
        jax.ShapeDtypeStruct((half_rows, width), f32),
        jax.ShapeDtypeStruct((half_rows, width), bf16),
    )

    def exchange(array, partners):
        return lax.all_to_all(array, "ctx", split_axis=0, concat_axis=0, axis_index_groups=partners, tiled=True)

    pieces = exchange(partial, lines)
    kept, given = call(
        merge_project,
        halves,
        pieces,
        w_vo,
        scratch=[VMEM((total_rows, latent), f32), VMEM((2, half_rows, width), f32)],
    )
    columns = call(combine, strip_shape, kept, swap(given), send_order)
    projected, hidden_state, normed = call(
        norm_rows,
        (
            jax.ShapeDtypeStruct((rows, width), f32),
            jax.ShapeDtypeStruct((rows, width), f32),
            strip_shape,
        ),
        exchange(columns, same_core),
        residual,
        norm_gain,
        scratch=[VMEM((8, width), f32), VMEM((height, strip), f32)],
    )
    inputs = exchange(normed, same_core)
    kept, given = call(
        functools.partial(run_expert, rows),
        halves,
        inputs,
        swap(inputs),
        back_order,
        expert_ids.T,
        route_weight.T,
        w_gate[0],
        w_up[0],
        w_down[0],
    )
    results = call(combine, strip_shape, kept, swap(given), send_order)
    attn_out, layer_out = call(
        add_mixture,
        (jax.ShapeDtypeStruct((rows, width), bf16), jax.ShapeDtypeStruct((rows, width), bf16)),
        exchange(results, same_core),
        hidden_state,
        projected,
        scratch=[VMEM((8, width), f32)],
    )
    return attn_out, layer_out


def fits(mesh, query_rope, residual, cache_latent, cache_rope):
    devices = mesh.shape["ctx"]
    rope_dim = cache_rope.shape[0] // mesh.shape["groups"]
    heads = query_rope.shape[1] // rope_dim
    rows = residual.shape[0] // (devices * mesh.shape["groups"])
    per = rows * heads // share
    return (
        heads == devices
        and devices % (2 * share) == 0
        and rope_dim == 64
        and 2 * per % 8 == 0
        and 8 <= per <= 16
        and rows * devices % 16 == 0
        and rows * devices <= 128
        and cache_latent.shape[1] == 512
        and cache_latent.shape[0] // (devices * mesh.shape["groups"]) == 512
        and devices & (devices - 1) == 0
        and residual.shape[1] % strip == 0
    )


def solution(mesh):
    in_specs = (
        P(("groups", "ctx"), None),
        P(("groups", "ctx"), None),
        P(("groups", "ctx"), None),
        P("groups", "ctx"),
        P("groups"),
        P("ctx", None),
        P(("groups", "ctx"), None),
        P(),
        P("groups", None),
        P("groups", None),
        P("ctx", None, None),
        P("ctx", None, None),
        P("ctx", None, None),
    )
    out_specs = (P(("groups", "ctx"), None), P(("groups", "ctx"), None))

    def layer(*args):
        kernels = fits(mesh, args[1], args[6], args[2], args[3])

        def body(*shards):
            return (kernel_layer if kernels else plain_layer)(*shards)

        step = jax.shard_map(body, mesh=mesh, in_specs=in_specs, out_specs=out_specs, check_vma=False)
        return step(*args)

    return layer
```
